256 devices in a mesh: branch: 4 (over x_hi, core), ty: 8 (over x_lo, y), tx: 8 (over z).
Axes of the slice: x: 4 (x_hi: 2, x_lo: 2; x = x_hi * 2 + x_lo), y: 4, z: 8, core: 2. Of those that a mesh axis runs over, the one named last changes fastest.
Arguments:
- feat0: bfloat16 [48, 512, 512], P(None, 'ty', 'tx'), may hold values from -6 to 6
- feat1: bfloat16 [96, 256, 256], P(None, 'ty', 'tx'), may hold values from -6 to 6
- feat2: bfloat16 [192, 128, 128], P(None, 'ty', 'tx'), may hold values from -6 to 6
- feat3: bfloat16 [384, 64, 64], P(None, 'ty', 'tx'), may hold values from -6 to 6
- block_w0: bfloat16 [2, 48, 432], replicated, may hold values from -0.3125 to 0.3125
- block_w1: bfloat16 [2, 96, 864], replicated, may hold values from -0.21875 to 0.21875
- block_w2: bfloat16 [2, 192, 1728], replicated, may hold values from -0.15625 to 0.15625
- block_w3: bfloat16 [2, 384, 3456], replicated, may hold values from -0.109375 to 0.109375
- block_b0: float32 [2, 48], replicated, may hold values from -1.8 to 1.8
- block_b1: float32 [2, 96], replicated, may hold values from -1.8 to 1.8
- block_b2: float32 [2, 192], replicated, may hold values from -1.8 to 1.8
- block_b3: float32 [2, 384], replicated, may hold values from -1.8 to 1.8
- up_w1: bfloat16 [1, 48, 96], replicated, may hold values from -0.625 to 0.625
- up_w2: bfloat16 [1, 144, 192], replicated, may hold values from -0.4375 to 0.4375
- up_w3: bfloat16 [1, 336, 384], replicated, may hold values from -0.3125 to 0.3125
- down_mid0: bfloat16 [1, 3, 48, 432], replicated, may hold values from -0.3125 to 0.3125
- down_mid1: bfloat16 [1, 1, 96, 864], replicated, may hold values from -0.21875 to 0.21875
- down_fin0: bfloat16 [1, 672, 432], replicated, may hold values from -0.3125 to 0.3125
- down_fin1: bfloat16 [1, 576, 864], replicated, may hold values from -0.21875 to 0.21875
- down_fin2: bfloat16 [1, 384, 1728], replicated, may hold values from -0.15625 to 0.15625
Outputs:
- joined0: bfloat16 [48, 512, 512], P(None, 'ty', 'tx')
- joined1: bfloat16 [96, 256, 256], P(None, 'ty', 'tx')
- joined2: bfloat16 [192, 128, 128], P(None, 'ty', 'tx')
- joined3: bfloat16 [384, 64, 64], P(None, 'ty', 'tx')
The draws below stay inside these ranges and needn't reach their ends.
All inputs are finite; a program needn't handle non-finite values.
Results may differ from the reference program's by a relative error of at most 0.0095.
Values may be sent and summed in bfloat16 or wider, within the bound.
No kernel may reach another device: no remote copies, remote signals or barrier semaphores. Data moves between devices by JAX's collectives and lax.ppermute only.
A program may use at most 128 MiB of HBM per device.

```python
import jax
import jax.numpy as jnp

CHAN = 48
MODULES = 1
BLOCKS = 1
CONVS = 2
HEIGHT = 512
WIDTH = 512


def shard_levels(own_key, shape, split, smallest, top_value):
    level, own = 1.0, jax.random.fold_in(own_key, 6)
    for axis_at, shards_of in split:
        draws = jnp.exp(jax.random.uniform(jax.random.fold_in(own, axis_at), (shards_of,), jnp.float32, smallest / len(split), top_value / len(split)))
        level = level * jnp.repeat(draws, shape[axis_at] // shards_of).reshape([-1 if axis == axis_at else 1 for axis in range(len(shape))])
    return level


def normal_values(rng, dims, scale, most, cuts=(), kind=jnp.bfloat16):
    values = scale * jax.random.normal(rng, dims, jnp.float32)
    if cuts:
        values = values * shard_levels(rng, dims, cuts, -0.22, 0.18)
    return jnp.clip(values, -most, most).astype(kind)


def setup_inputs(seed: int = 0) -> dict:
    key_of = jax.random.split(jax.random.key(seed), 21)
    feat0 = normal_values(key_of[0], (CHAN, HEIGHT, WIDTH), 1.0, 6.0, ((1, 8), (2, 8)))
    feat1 = normal_values(key_of[1], (2 * CHAN, HEIGHT // 2, WIDTH // 2), 1.0, 6.0, ((1, 8), (2, 8)))
    feat2 = normal_values(key_of[2], (4 * CHAN, HEIGHT // 4, WIDTH // 4), 1.0, 6.0, ((1, 8), (2, 8)))
    feat3 = normal_values(key_of[3], (8 * CHAN, HEIGHT // 8, WIDTH // 8), 1.0, 6.0, ((1, 8), (2, 8)))
    block_w0 = normal_values(key_of[4], (CONVS, CHAN, 9 * CHAN), (9 * CHAN) ** -0.5, 0.3125)
    block_w1 = normal_values(key_of[5], (CONVS, 2 * CHAN, 18 * CHAN), (18 * CHAN) ** -0.5, 0.21875)
    block_w2 = normal_values(key_of[6], (CONVS, 4 * CHAN, 36 * CHAN), (36 * CHAN) ** -0.5, 0.15625)
    block_w3 = normal_values(key_of[7], (CONVS, 8 * CHAN, 72 * CHAN), (72 * CHAN) ** -0.5, 0.109375)
    block_b0 = normal_values(key_of[8], (CONVS, CHAN), 0.3, 1.8, (), jnp.float32)
    block_b1 = normal_values(key_of[9], (CONVS, 2 * CHAN), 0.3, 1.8, (), jnp.float32)
    block_b2 = normal_values(key_of[10], (CONVS, 4 * CHAN), 0.3, 1.8, (), jnp.float32)
    block_b3 = normal_values(key_of[11], (CONVS, 8 * CHAN), 0.3, 1.8, (), jnp.float32)
    up_w1 = normal_values(key_of[12], (MODULES, CHAN, 2 * CHAN), (2 * CHAN) ** -0.5, 0.625)
    up_w2 = normal_values(key_of[13], (MODULES, 3 * CHAN, 4 * CHAN), (4 * CHAN) ** -0.5, 0.4375)
    up_w3 = normal_values(key_of[14], (MODULES, 7 * CHAN, 8 * CHAN), (8 * CHAN) ** -0.5, 0.3125)
    down_mid0 = normal_values(key_of[15], (MODULES, 3, CHAN, 9 * CHAN), (9 * CHAN) ** -0.5, 0.3125)
    down_mid1 = normal_values(key_of[16], (MODULES, 1, 2 * CHAN, 18 * CHAN), (18 * CHAN) ** -0.5, 0.21875)
    down_fin0 = normal_values(key_of[17], (MODULES, 14 * CHAN, 9 * CHAN), (9 * CHAN) ** -0.5, 0.3125)
    down_fin1 = normal_values(key_of[18], (MODULES, 12 * CHAN, 18 * CHAN), (18 * CHAN) ** -0.5, 0.21875)
    down_fin2 = normal_values(key_of[19], (MODULES, 8 * CHAN, 36 * CHAN), (36 * CHAN) ** -0.5, 0.15625)
    return {"feat0": feat0, "feat1": feat1, "feat2": feat2, "feat3": feat3, "block_w0": block_w0, "block_w1": block_w1, "block_w2": block_w2, "block_w3": block_w3, "block_b0": block_b0, "block_b1": block_b1, "block_b2": block_b2, "block_b3": block_b3, "up_w1": up_w1, "up_w2": up_w2, "up_w3": up_w3, "down_mid0": down_mid0, "down_mid1": down_mid1, "down_fin0": down_fin0, "down_fin1": down_fin1, "down_fin2": down_fin2}


def convolve(feature, weight, stride):
    channels, height, breadth = feature.shape
    padded = jnp.pad(feature, ((0, 0), (1, 1), (1, 1)))
    out_height = height // stride
    out_breadth = breadth // stride
    running = jnp.zeros((weight.shape[0], out_height * out_breadth), jnp.float32)
    for tap_index in range(9):
        row_tap, col_tap = divmod(tap_index, 3)
        window = padded[:, row_tap:row_tap + stride * (out_height - 1) + 1:stride, col_tap:col_tap + stride * (out_breadth - 1) + 1:stride]
        window = window.reshape(channels, out_height * out_breadth)
        running = running + jnp.dot(weight[:, tap_index * channels:(tap_index + 1) * channels], window, preferred_element_type=jnp.float32)
    return running.reshape(weight.shape[0], out_height, out_breadth)


def residual_block(feature, first_weight, first_bias, second_weight, second_bias):
    inner = jax.nn.relu(convolve(feature, first_weight, 1) + first_bias[:, None, None]).astype(jnp.bfloat16)
    summed = feature.astype(jnp.float32) + convolve(inner, second_weight, 1) + second_bias[:, None, None]
    return jax.nn.relu(summed).astype(jnp.bfloat16)


def joining_terms(source, source_id, module_id, channels, up_weights, mid_weights, final_weights):
    result = []
    up_offset = 0
    down_offset = 0
    mid_count = 0
    if source_id > 0:
        lifted = jnp.dot(up_weights[source_id][module_id], source.reshape(source.shape[0], -1), preferred_element_type=jnp.float32)
    for target in range(4):
        if target == source_id:
            result.append(source)
        elif target < source_id:
            part = lifted[up_offset:up_offset + channels[target]].astype(jnp.bfloat16)
            up_offset = up_offset + channels[target]
            part = part.reshape(channels[target], source.shape[1], source.shape[2])
            factor = 2 ** (source_id - target)
            part = jnp.repeat(jnp.repeat(part, factor, axis=1), factor, axis=2)
            result.append(part)
        else:
            value = source
            for step_id in range(target - source_id - 1):
                value = jax.nn.relu(convolve(value, mid_weights[source_id][module_id, mid_count], 2)).astype(jnp.bfloat16)
                mid_count = mid_count + 1
            rows_used = final_weights[source_id][module_id, down_offset:down_offset + channels[target]]
            down_offset = down_offset + channels[target]
            result.append(convolve(value, rows_used, 2).astype(jnp.bfloat16))
    return result


def reference(feat0, feat1, feat2, feat3, block_w0, block_w1, block_w2, block_w3, block_b0, block_b1, block_b2, block_b3, up_w1, up_w2, up_w3, down_mid0, down_mid1, down_fin0, down_fin1, down_fin2):
    features = [feat0, feat1, feat2, feat3]
    block_weights = (block_w0, block_w1, block_w2, block_w3)
    block_biases = (block_b0, block_b1, block_b2, block_b3)
    up_weights = (None, up_w1, up_w2, up_w3)
    mid_weights = (down_mid0, down_mid1, None, None)
    final_weights = (down_fin0, down_fin1, down_fin2, None)
    channels = [feature.shape[0] for feature in features]
    for module_id in range(MODULES):
        sources = []
        for branch_id in range(4):
            source = features[branch_id]
            for block_id in range(BLOCKS):
                first_conv = (module_id * BLOCKS + block_id) * 2
                source = residual_block(source, block_weights[branch_id][first_conv], block_biases[branch_id][first_conv], block_weights[branch_id][first_conv + 1], block_biases[branch_id][first_conv + 1])
            sources.append(source)
        totals = [jnp.zeros(feature.shape, jnp.float32) for feature in features]
        for source_id in range(4):
            term_list = joining_terms(sources[source_id], source_id, module_id, channels, up_weights, mid_weights, final_weights)
            totals = [running + term.astype(jnp.float32) for running, term in zip(totals, term_list)]
        features = [jax.nn.relu(running).astype(jnp.bfloat16) for running in totals]
    return (features[0], features[1], features[2], features[3])
```

```python
import functools

import jax
import jax.numpy as jnp
from jax import lax
from jax.experimental import pallas as pl
from jax.experimental.pallas import tpu as pltpu
from jax.sharding import PartitionSpec as P

BF = jnp.bfloat16
F32 = jnp.float32
TILE = (64, 32, 16, 8)
CHAN = (48, 96, 192, 384)
LEAD = (9, 5, 3, 2)
EXT = (75, 39, 21, 12)
PITCH = (80, 48, 32, 16)
TALL = (80, 48, 32, 16)
GROUP = (16, 16, 16, 8)
DOWN_ROWS, UP_ROWS = 592, 240
RIGHT_ROWS, LEFT_ROWS = 928, 400
PARAMS = pltpu.CompilerParams(vmem_limit_bytes=56 * 2**20)


def spans(chan):
    return [(lo, min(lo + 128, chan)) for lo in range(0, chan, 128)]


def put_packed(ref, at, value, branch, split):
    if branch == 0:
        ref[at : at + split, 0:48] = value[:split]
        ref[at : at + value.shape[0] - split, 64:112] = value[split:]
        return at + split
    for lo, hi in spans(CHAN[branch]):
        ref[at : at + value.shape[0], 0 : hi - lo] = value[:, lo:hi]
        at += value.shape[0]
    return at


def take_packed(ref, at, count, branch, split):
    if branch == 0:
        return jnp.concatenate(
            [ref[at : at + split, 0:48], ref[at : at + count - split, 64:112]], axis=0
        ), at + split
    parts = []
    for lo, hi in spans(CHAN[branch]):
        parts.append(ref[at : at + count, 0 : hi - lo])
        at += count
    return (parts[0] if len(parts) == 1 else jnp.concatenate(parts, axis=1)), at


def flat_rows(ref, lo, hi, branch):
    side = TILE[branch]
    value = ref[lo:hi].astype(F32)
    return value.reshape((hi - lo) * side, CHAN[branch]).astype(BF)


def pack_rows(f0, f1, f2, f3, down, up):
    at = 0
    for b, f in enumerate((f0, f1, f2, f3)):
        at = put_packed(down, at, flat_rows(f, TILE[b] - LEAD[b], TILE[b], b), b, 288)
    at = 0
    for b, f in enumerate((f0, f1, f2, f3)):
        at = put_packed(up, at, flat_rows(f, 0, 2, b), b, 64)


def pack_cols(f0, f1, f2, f3, above, below, right, left, work):
    down_at = up_at = right_at = left_at = 0
    for b, f in enumerate((f0, f1, f2, f3)):
        side, lead, chan, group = TILE[b], LEAD[b], CHAN[b], GROUP[b]
        high, down_at = take_packed(above, down_at, lead * side, b, 288)
        low, up_at = take_packed(below, up_at, 2 * side, b, 64)
        parts = (
            (high.astype(F32).reshape(lead, side, chan), 0, lead),
            (f[...].astype(F32).reshape(side, side, chan), lead, side),
            (low.astype(F32).reshape(2, side, chan), lead + side, 2),
        )
        for last in (True, False):
            cut = slice(side - group, side) if last else slice(0, group)
            for value, start, count in parts:
                edge = value[:, cut].reshape(count * group, chan)
                for s, (lo, hi) in enumerate(spans(chan)):
                    work[s, start * group : (start + count) * group, 0 : hi - lo] = edge[:, lo:hi]
            columns = range(group - lead, group) if last else range(2)
            cols = []
            for k in columns:
                planes = [
                    work[s, pl.ds(k, TALL[b], stride=group), 0 : hi - lo]
                    for s, (lo, hi) in enumerate(spans(chan))
                ]
                cols.append([p.astype(BF) for p in planes])
            target, at = (right, right_at) if last else (left, left_at)
            if b == 0:
                half = 5 if last else 1
                for i, (col,) in enumerate(cols):
                    place = at + (i if i < half else i - half) * TALL[0]
                    lane = 0 if i < half else 64
                    target[place : place + TALL[0], lane : lane + 48] = col
                at += half * TALL[0]
            else:
                for s, (lo, hi) in enumerate(spans(chan)):
                    for col in cols:
                        target[at : at + TALL[b], 0 : hi - lo] = col[s]
                        at += TALL[b]
            if last:
                right_at = at
            else:
                left_at = at


def clear_edges(place, planes, pitch, height, breadth, lead, trail):
    ty, tx = place[0], place[1]

    def rows(lo, count):
        for ref in planes:
            ref[lo * pitch : (lo + count) * pitch] = jnp.zeros((count * pitch, ref.shape[1]), F32)

    def cols(lo, count):
        for ref in planes:
            for k in range(lo, lo + count):
                ref[pl.ds(k, height, stride=pitch), :] = jnp.zeros((height, ref.shape[1]), F32)

    if lead:
        pl.when(ty == 0)(lambda: rows(0, lead))
        pl.when(tx == 0)(lambda: cols(0, lead))
    if trail:
        pl.when(ty == 7)(lambda: rows(height - trail, trail))
        pl.when(tx == 7)(lambda: cols(breadth - trail, trail))


def dot_nt(x, w):
    return lax.dot_general(x, w, (((1,), (1,)), ((), ())), preferred_element_type=F32)


def rounded(x):
    return x.astype(BF).astype(F32)


def main(
    place, f0, f1, f2, f3, above, below, cl, cr,
    w0, w1, w2, w3, b0, b1, b2, b3, u1, u2, u3, d01, d02, d12, fin03, fin13, fin23,
    j0, j1, j2, j3,
    x0, h0, a0, s0, t0, v01, v0, t02w, vv02, n03,
    x1, h1, a1, s1, t1, vv12, m13,
    x2, h2, a2, s2,
    x3, h3, a3, s3,
    z1, z2, y2, y1, wide, mcol,
):
    feats = (f0, f1, f2, f3)
    xs = ([x0], [x1], [x2.at[0], x2.at[1]], [x3.at[i] for i in range(3)])
    hs = ([h0], [h1], [h2.at[0], h2.at[1]], [h3.at[i] for i in range(3)])
    as_ = ([a0], [a1], [a2.at[0], a2.at[1]], [a3.at[i] for i in range(3)])
    x1[:, 96:128] = jnp.zeros((x1.shape[0], 32), F32)
    h1[:, 96:128] = jnp.zeros((h1.shape[0], 32), F32)
    a1[:, 96:128] = jnp.zeros((a1.shape[0], 32), F32)
    s0[...] = jnp.zeros_like(s0)
    t0[...] = jnp.zeros_like(t0)
    s2[...] = jnp.zeros_like(s2)

    def assemble(b, ats):
        side, lead, chan, pitch = TILE[b], LEAD[b], CHAN[b], PITCH[b]
        down_at, up_at, right_at, left_at = ats
        high, down_at = take_packed(above, down_at, lead * side, b, 288)
        low, up_at = take_packed(below, up_at, 2 * side, b, 64)
        for value, start, count in ((high, 0, lead), (low, lead + side, 2)):
            for y in range(count):
                row = value[y * side : (y + 1) * side].astype(F32)
                for s, (lo, hi) in enumerate(spans(chan)):
                    xs[b][s][pl.ds((start + y) * pitch + lead, side), 0 : hi - lo] = row[:, lo:hi]

        for y in range(side):
            row = feats[b][y].astype(F32)
            for s, (lo, hi) in enumerate(spans(chan)):
                xs[b][s][pl.ds((lead + y) * pitch + lead, side), 0 : hi - lo] = row[:, lo:hi]
        for ref, at, count, first, half in ((cl, right_at, lead, 0, 5), (cr, left_at, 2, lead + side, 1)):
            if b == 0:
                for i in range(count):
                    spot = at + (i if i < half else i - half) * TALL[0]
                    lane = 0 if i < half else 64
                    col = ref[spot : spot + TALL[0], lane : lane + 48].astype(F32)
                    x0[pl.ds(first + i, EXT[0], stride=pitch), 0:48] = col[: EXT[0]]
                at += half * TALL[0]
            else:
                for s, (lo, hi) in enumerate(spans(chan)):
                    for i in range(count):
                        col = ref[at : at + TALL[b], 0 : hi - lo].astype(F32)
                        xs[b][s][pl.ds(first + i, EXT[b], stride=pitch), 0 : hi - lo] = col[: EXT[b]]
                        at += TALL[b]
            if ref is cl:
                right_at = at
            else:
                left_at = at
        clear_edges(place, xs[b], pitch, EXT[b], EXT[b], lead, 2)
        return down_at, up_at, right_at, left_at

    ats = (0, 0, 0, 0)
    for b in range(4):
        ats = assemble(b, ats)

    def spread(planes, target, rows, step, slot, chan, lanes):
        @pl.loop(0, rows // step)
        def _(i):
            p = pl.multiple_of(i * step, step)
            for dx in range(3):
                for s, (lo, hi) in enumerate(spans(lanes)):
                    piece = planes[s][pl.ds(p + dx, step), 0 : hi - lo].astype(BF)
                    target[pl.ds(p, step), dx * slot + lo : dx * slot + hi] = piece

    def conv_loop(source, weight, rows, step, pitch, width, finish):
        @pl.loop(0, rows // step)
        def _(i):
            p = pl.multiple_of(i * step, step)
            total = None
            for dy in range(3):
                part = dot_nt(source[pl.ds(p + dy * pitch, step), 0:width], weight(dy))
                total = part if total is None else total + part
            finish(p, total)

    def block(b, weight, bias, source, slot, lanes, width, inner_rows, outer_rows, step, copy_step):
        pitch, chan, lead = PITCH[b], CHAN[b], LEAD[b]

        def inner(p, total):
            value = jnp.maximum(total + bias[0:1, :], 0.0)
            for s, (lo, hi) in enumerate(spans(chan)):
                hs[b][s][pl.ds(p, step), 0 : hi - lo] = value[:, lo:hi]

        def outer(p, total):
            total = total + bias[1:2, :]
            for s, (lo, hi) in enumerate(spans(chan)):
                kept = xs[b][s][pl.ds(p + 2 * pitch + 2, step), 0 : hi - lo]
                value = rounded(jnp.maximum(kept + total[:, lo:hi], 0.0))
                as_[b][s][pl.ds(p, step), 0 : hi - lo] = value

        spread(xs[b], source, inner_rows + 2 * pitch, copy_step, slot, chan, lanes)
        conv_loop(source, lambda dy: weight(0, dy), inner_rows, step, pitch, width, inner)
        clear_edges(place, hs[b], pitch, EXT[b] - 2, EXT[b] - 2, lead - 1, 1)
        spread(hs[b], source, outer_rows + 2 * pitch, copy_step, slot, chan, lanes)
        conv_loop(source, lambda dy: weight(1, dy), outer_rows, step, pitch, width, outer)
        clear_edges(place, as_[b], pitch, EXT[b] - 4, EXT[b] - 4, lead - 2, 0)

    block(0, lambda i, dy: w0[i, dy], b0, s0, 64, 48, 192, 76 * 80, 72 * 80, 320, 160)
    block(1, lambda i, dy: w1[i, dy], b1, s1, 128, 128, 384, 40 * 48, 36 * 48, 192, 96)
    block(2, lambda i, dy: w2[i, dy], b2, s2, 256, 192, 704, 20 * 32, 20 * 32, 160, 32)
    block(
        3,
        lambda i, dy: w3[i, :, dy * 1152 : (dy + 1) * 1152],
        b3, s3, 384, 384, 1152, 10 * 16, 10 * 16, 160, 16,
    )

    @pl.loop(0, 37)
    def _(r):
        for par in range(2):
            for dx in range(3):
                piece = a0[pl.ds((2 * r + par) * 80 + dx, 48, stride=2), 0:48]
                t0[par, pl.ds(pl.multiple_of(r * 48, 48), 48), dx * 64 : dx * 64 + 48] = piece.astype(BF)

    @pl.loop(0, 9)
    def _(i):
        p = pl.multiple_of(i * 192, 192)
        total = None
        for dy in range(3):
            part = dot_nt(t0[dy % 2, pl.ds(p + (dy // 2) * 48, 192), 0:192], d01[dy])
            total = part if total is None else total + part
        v01[pl.ds(p, 192), :] = rounded(total[:, :128])
        v0[pl.ds(p, 192), :] = rounded(jnp.maximum(total[:, 128:], 0.0))

    clear_edges(place, [v0], 48, 35, 35, 3, 0)

    @pl.loop(0, 18)
    def _(r):
        for par in range(2):
            for dx in range(3):
                piece = v0[pl.ds((2 * r + par) * 48 + dx, 32, stride=2), :]
                t02w[par, pl.ds(pl.multiple_of(r * 32, 32), 32), dx * 128 : dx * 128 + 128] = piece.astype(BF)
                piece = a1[pl.ds((2 * r + par) * 48 + dx, 32, stride=2), :]
                t1[par, pl.ds(pl.multiple_of(r * 32, 32), 32), dx * 128 : dx * 128 + 128] = piece.astype(BF)

    for p, n in ((0, 288), (288, 256)):
        total = other = None
        for dy in range(3):
            cut = pl.ds(p + (dy // 2) * 32, n)
            part = dot_nt(t02w[dy % 2, cut, :], d02[dy])
            total = part if total is None else total + part
            part = dot_nt(t1[dy % 2, cut, :], d12[dy])
            other = part if other is None else other + part
        vv02[0, p : p + n, :] = rounded(total[:, :128])
        vv02[1, p : p + n, 0:64] = rounded(total[:, 128:192])
        n03[p : p + n, :] = rounded(jnp.maximum(total[:, 192:240], 0.0))
        vv12[0, p : p + n, :] = rounded(other[:, :128])
        vv12[1, p : p + n, 0:64] = rounded(other[:, 128:192])
        m13[p : p + n, :] = rounded(jnp.maximum(other[:, 256:352], 0.0))

    clear_edges(place, [n03], 32, 17, 17, 1, 0)
    clear_edges(place, [m13], 32, 17, 17, 1, 0)

    def gathered(ref, width, dy, dx):
        return jnp.concatenate(
            [ref[pl.ds((2 * i + dy) * 32 + dx, 8, stride=2), 0:width] for i in range(8)], axis=0
        ).astype(BF)

    t03 = t13 = t23 = None
    for tap in range(9):
        dy, dx = divmod(tap, 3)
        part = dot_nt(gathered(n03, 48, dy, dx), fin03[tap])
        t03 = part if t03 is None else t03 + part
        part = dot_nt(gathered(m13, 96, dy, dx), fin13[tap])
        t13 = part if t13 is None else t13 + part
        for s, (lo, hi) in enumerate(spans(192)):
            part = jnp.dot(
                gathered(a2.at[s], hi - lo, dy, dx),
                fin23[tap * 192 + lo : tap * 192 + hi, :],
                preferred_element_type=F32,
            )
            t23 = part if t23 is None else t23 + part

    c3 = [
        jnp.concatenate([a3[s, y * 16 : y * 16 + 8, :] for y in range(8)], axis=0) for s in range(3)
    ]
    c3 = jnp.concatenate(c3, axis=1)
    three = jnp.maximum(c3 + rounded(t03) + rounded(t13) + rounded(t23), 0.0)
    j3[...] = three.reshape(8, 8, 384).astype(BF)

    c3b = c3.astype(BF)
    t30 = rounded(dot_nt(c3b, u3[0:48, :]))
    t31 = rounded(dot_nt(c3b, u3[48:144, :]))
    t32 = rounded(dot_nt(c3b, u3[144:336, :]))
    c2 = [
        jnp.concatenate([a2[s, pl.ds((y + 1) * 32 + 1, 16), 0 : hi - lo] for y in range(16)], axis=0)
        for s, (lo, hi) in enumerate(spans(192))
    ]
    c2 = jnp.concatenate(c2, axis=1)
    c2b = c2.astype(BF)
    t20 = rounded(dot_nt(c2b, u2[0:48, :]))
    t21 = rounded(dot_nt(c2b, u2[48:144, :]))

    def doubled(target, small, side, lanes):
        for y in range(side):
            row = small[y * side : (y + 1) * side]
            for odd in range(2):
                for right in range(2):
                    target[pl.ds((2 * y + odd) * 2 * side + right, side, stride=2), 0:lanes] = row

    for s, (lo, hi) in enumerate(spans(192)):
        doubled(wide, t32[:, lo:hi], 8, hi - lo)
        for y in range(16):
            t02 = vv02[s, pl.ds((y + 1) * 32 + 1, 16), 0 : hi - lo]
            t12 = vv12[s, pl.ds((y + 1) * 32 + 1, 16), 0 : hi - lo]
            keep = c2[y * 16 : (y + 1) * 16, lo:hi]
            row = keep + t02 + t12 + wide[pl.ds(y * 16, 16), 0 : hi - lo]
            j2[y, :, lo:hi] = jnp.maximum(row, 0.0).astype(BF)

    doubled(z2, t30, 8, 48)
    sum2 = z2[...] + t20
    doubled(z1, sum2, 16, 48)
    doubled(y2, t31, 8, 96)
    sum2 = y2[...] + t21
    doubled(y1, sum2, 16, 96)

    @pl.loop(0, 32)
    def _(y):
        one = a1[pl.ds((y + 3) * 48 + 3, 32), 0:96]
        t01 = v01[pl.ds((y + 3) * 48 + 3, 32), 0:96]
        spot = pl.ds(pl.multiple_of(y * 32, 32), 32)
        j1[y] = jnp.maximum(one + t01 + y1[spot, :], 0.0).astype(BF)
        row = rounded(dot_nt(one.astype(BF), u1[...])) + z1[spot, :]
        for right in range(2):
            mcol[pl.ds(right, 32, stride=2), :] = row
        for odd in range(2):
            zero = a0[pl.ds((2 * y + odd + 7) * 80 + 7, 64), 0:48]
            j0[2 * y + odd] = jnp.maximum(zero + mcol[...], 0.0).astype(BF)


def ring(x, axis, by):
    n = lax.axis_size(axis)
    return lax.ppermute(x, axis, [(i, (i + by) % n) for i in range(n)])


def shape(*dims, kind=BF):
    return jax.ShapeDtypeStruct(dims, kind)


def slotted(w, chan, slot):
    taps = w.reshape(w.shape[0], 3, 3, chan).transpose(1, 0, 2, 3)
    taps = jnp.pad(taps, ((0, 0), (0, 0), (0, 0), (0, slot - chan)))
    return taps.reshape(3, w.shape[0], 3 * slot)


def tapped(w, chan):
    return w.reshape(w.shape[0], 9, chan).transpose(1, 0, 2)


def padded_rows(w, rows):
    return jnp.pad(w, ((0, rows - w.shape[0]), (0, 0)))


def per_device(
    feat0, feat1, feat2, feat3,
    block_w0, block_w1, block_w2, block_w3,
    block_b0, block_b1, block_b2, block_b3,
    up_w1, up_w2, up_w3,
    down_mid0, down_mid1, down_fin0, down_fin1, down_fin2,
):
    maps = [f.transpose(1, 2, 0) for f in (feat0, feat1, feat2, feat3)]
    down, up = pl.pallas_call(
        pack_rows,
        out_shape=[shape(DOWN_ROWS, 128), shape(UP_ROWS, 128)],
        compiler_params=PARAMS,
    )(*maps)
    above, below = ring(down, "ty", 1), ring(up, "ty", -1)
    right, left = pl.pallas_call(
        pack_cols,
        out_shape=[shape(RIGHT_ROWS, 128), shape(LEFT_ROWS, 128)],
        scratch_shapes=[pltpu.VMEM((3, 80 * 16, 128), F32)],
        compiler_params=PARAMS,
    )(*maps, above, below)
    cl, cr = ring(right, "tx", 1), ring(left, "tx", -1)

    w0 = jnp.stack([slotted(block_w0[i], 48, 64) for i in range(2)])
    w1 = jnp.stack([slotted(block_w1[i], 96, 128) for i in range(2)])
    w2 = jnp.stack([slotted(block_w2[i], 192, 256)[:, :, :704] for i in range(2)])
    fin0, mid0 = down_fin0[0], down_mid0[0]
    d01 = slotted(
        jnp.concatenate(
            [padded_rows(fin0[:96], 128), padded_rows(mid0[0], 64), padded_rows(mid0[1], 64)]
        ),
        48,
        64,
    )
    taps = fin0[96:288].reshape(192, 9, 48)
    inner = mid0[2].reshape(48, 9, 48)
    d02 = jnp.concatenate(
        [
            jnp.pad(taps, ((0, 0), (0, 0), (0, 80))),
            jnp.pad(inner, ((0, 16), (0, 0), (64, 16))),
        ]
    ).reshape(256, 3, 384).transpose(1, 0, 2)
    d12 = slotted(
        jnp.concatenate([padded_rows(down_fin1[0, :192], 256), down_mid1[0, 0]]), 96, 128
    )
    fin03 = tapped(fin0[288:], 48)
    fin13 = tapped(down_fin1[0, 192:], 96)
    fin23 = down_fin2[0].T
    place = jnp.stack([lax.axis_index("ty"), lax.axis_index("tx")]).astype(jnp.int32)

    vmem = pl.BlockSpec(memory_space=pltpu.VMEM)
    f32 = lambda *dims: pltpu.VMEM(dims, F32)
    bf = lambda *dims: pltpu.VMEM(dims, BF)
    outs = pl.pallas_call(
        main,
        out_shape=[shape(64, 64, 48), shape(32, 32, 96), shape(16, 16, 192), shape(8, 8, 384)],
        in_specs=[pl.BlockSpec(memory_space=pltpu.SMEM)] + [vmem] * 25,
        scratch_shapes=[
            f32(6416, 48), f32(6320, 48), f32(6064, 48), bf(6400, 256), bf(2, 38 * 48, 192),
            f32(1728, 128), f32(1840, 128), bf(2, 19 * 32, 384), f32(2, 544, 128), f32(600, 48),
            f32(2080, 128), f32(2032, 128), f32(1840, 128), bf(2048, 384), bf(2, 19 * 32, 384),
            f32(2, 544, 128), f32(600, 96),
            f32(2, 768, 128), f32(2, 768, 128), f32(2, 704, 128), bf(768, 768),
            f32(3, 224, 128), f32(3, 224, 128), f32(3, 176, 128), bf(208, 1152),
            f32(1024, 48), f32(256, 48), f32(256, 96), f32(1024, 96), f32(256, 128), f32(64, 48),
        ],
        compiler_params=PARAMS,
    )(
        place, *maps, above, below, cl, cr,
        w0, w1, w2, block_w3, block_b0, block_b1, block_b2, block_b3,
        up_w1[0], up_w2[0], up_w3[0], d01, d02, d12, fin03, fin13, fin23,
    )
    return tuple(o.transpose(2, 0, 1) for o in outs)


def solution(mesh):
    tile = P(None, "ty", "tx")
    return jax.shard_map(
        per_device,
        mesh=mesh,
        in_specs=(tile,) * 4 + (P(),) * 16,
        out_specs=(tile,) * 4,
        check_vma=False,
    )
```

```python
import functools

import jax
import jax.numpy as jnp
from jax import lax
from jax.experimental import pallas as pl
from jax.experimental.pallas import tpu as pltpu
from jax.sharding import PartitionSpec as P

BF = jnp.bfloat16
F32 = jnp.float32
TILE = (64, 32, 16, 8)
CHAN = (48, 96, 192, 384)
LEAD = (9, 5, 3, 2)
EXT = (75, 39, 21, 12)
PITCH = (80, 48, 32, 16)
TALL = (80, 48, 32, 16)
GROUP = (16, 16, 16, 8)
DOWN_ROWS, UP_ROWS = 592, 240
RIGHT_ROWS, LEFT_ROWS = 928, 400
PARAMS = pltpu.CompilerParams(vmem_limit_bytes=16 * 2**20)
MAIN_PARAMS = pltpu.CompilerParams(vmem_limit_bytes=56 * 2**20)


def spans(chan):
    return [(lo, min(lo + 128, chan)) for lo in range(0, chan, 128)]


def put_packed(ref, at, value, branch, split):
    if branch == 0:
        ref[at : at + split, 0:48] = value[:split]
        ref[at : at + value.shape[0] - split, 64:112] = value[split:]
        return at + split
    for lo, hi in spans(CHAN[branch]):
        ref[at : at + value.shape[0], 0 : hi - lo] = value[:, lo:hi]
        at += value.shape[0]
    return at


def take_packed(ref, at, count, branch, split):
    if branch == 0:
        return jnp.concatenate(
            [ref[at : at + split, 0:48], ref[at : at + count - split, 64:112]], axis=0
        ), at + split
    parts = []
    for lo, hi in spans(CHAN[branch]):
        parts.append(ref[at : at + count, 0 : hi - lo])
        at += count
    return (parts[0] if len(parts) == 1 else jnp.concatenate(parts, axis=1)), at


def flat_rows(ref, lo, hi, branch):
    side = TILE[branch]
    value = ref[lo:hi].astype(F32)
    return value.reshape((hi - lo) * side, CHAN[branch]).astype(BF)


def pack_rows(f0, f1, f2, f3, down, up):
    at = 0
    for b, f in enumerate((f0, f1, f2, f3)):
        at = put_packed(down, at, flat_rows(f, TILE[b] - LEAD[b], TILE[b], b), b, 288)
    at = 0
    for b, f in enumerate((f0, f1, f2, f3)):
        at = put_packed(up, at, flat_rows(f, 0, 2, b), b, 64)


def pack_cols(f0, f1, f2, f3, above, below, right, left, work):
    down_at = up_at = right_at = left_at = 0
    for b, f in enumerate((f0, f1, f2, f3)):
        side, lead, chan, group = TILE[b], LEAD[b], CHAN[b], GROUP[b]
        high, down_at = take_packed(above, down_at, lead * side, b, 288)
        low, up_at = take_packed(below, up_at, 2 * side, b, 64)
        parts = (
            (high.astype(F32).reshape(lead, side, chan), 0, lead),
            (f[...].astype(F32).reshape(side, side, chan), lead, side),
            (low.astype(F32).reshape(2, side, chan), lead + side, 2),
        )
        for last in (True, False):
            cut = slice(side - group, side) if last else slice(0, group)
            for value, start, count in parts:
                edge = value[:, cut].reshape(count * group, chan)
                for s, (lo, hi) in enumerate(spans(chan)):
                    work[s, start * group : (start + count) * group, 0 : hi - lo] = edge[:, lo:hi]
            columns = range(group - lead, group) if last else range(2)
            cols = []
            for k in columns:
                planes = [
                    work[s, pl.ds(k, TALL[b], stride=group), 0 : hi - lo]
                    for s, (lo, hi) in enumerate(spans(chan))
                ]
                cols.append([p.astype(BF) for p in planes])
            target, at = (right, right_at) if last else (left, left_at)
            if b == 0:
                half = 5 if last else 1
                for i, (col,) in enumerate(cols):
                    place = at + (i if i < half else i - half) * TALL[0]
                    lane = 0 if i < half else 64
                    target[place : place + TALL[0], lane : lane + 48] = col
                at += half * TALL[0]
            else:
                for s, (lo, hi) in enumerate(spans(chan)):
                    for col in cols:
                        target[at : at + TALL[b], 0 : hi - lo] = col[s]
                        at += TALL[b]
            if last:
                right_at = at
            else:
                left_at = at


def clear_edges(place, planes, pitch, height, breadth, lead, trail):
    ty, tx = place[0], place[1]

    def rows(lo, count):
        for ref in planes:
            ref[lo * pitch : (lo + count) * pitch] = jnp.zeros((count * pitch, ref.shape[1]), F32)

    def cols(lo, count):
        for ref in planes:
            for k in range(lo, lo + count):
                ref[pl.ds(k, height, stride=pitch), :] = jnp.zeros((height, ref.shape[1]), F32)

    if lead:
        pl.when(ty == 0)(lambda: rows(0, lead))
        pl.when(tx == 0)(lambda: cols(0, lead))
    if trail:
        pl.when(ty == 7)(lambda: rows(height - trail, trail))
        pl.when(tx == 7)(lambda: cols(breadth - trail, trail))


def dot_nt(x, w):
    return lax.dot_general(x, w, (((1,), (1,)), ((), ())), preferred_element_type=F32)


def rounded(x):
    return x.astype(BF).astype(F32)


def main(
    f0, f1, f2, f3, above, below, cl, cr,
    w0, b0, b1, b2, b3, u1, *rest,
):
    far, rest = rest[:10], rest[10:]
    outs, near, scratch = rest[:4], rest[4:14], rest[14:-1]
    main_body(
        f0, f1, f2, f3, above, below, cl, cr, w0, b0, b1, b2, b3, u1, far, near, rest[-1], *outs, *scratch
    )


def main_body(
    f0, f1, f2, f3, above, below, cl, cr, w0, b0, b1, b2, b3, u1, far, near, sems,
    j0, j1, j2, j3,
    x0, h0, a0, s0, t0, d01, v01, v0, ta, tb, vv02, n03, g03,
    x1, h1, a1, s1, t1, vv12, m13, g13,
    x2, h2, a2, s2, g23,
    x3, h3, a3, s3,
    z1, z2, y2, y1, wide, c1, mcol, jt,
):
    place = (lax.axis_index("ty"), lax.axis_index("tx"))
    copies = [pltpu.make_async_copy(a, b, sems.at[i]) for i, (a, b) in enumerate(zip(far, near))]
    for copy in copies:
        copy.start()
    w1, w2, w3, mid0, mid1, fin0, fin1, fin2, u3, u2 = near
    feats = (f0, f1, f2, f3)
    xs = ([x0], [x1], [x2.at[0], x2.at[1]], [x3.at[i] for i in range(3)])
    hs = ([h0], [h1], [h2.at[0], h2.at[1]], [h3.at[i] for i in range(3)])
    as_ = ([a0], [a1], [a2.at[0], a2.at[1]], [a3.at[i] for i in range(3)])

    def assemble(b, ats):
        side, lead, chan, pitch = TILE[b], LEAD[b], CHAN[b], PITCH[b]
        down_at, up_at, right_at, left_at = ats
        high, down_at = take_packed(above, down_at, lead * side, b, 288)
        low, up_at = take_packed(below, up_at, 2 * side, b, 64)
        for value, start, count in ((high, 0, lead), (low, lead + side, 2)):
            for y in range(count):
                row = value[y * side : (y + 1) * side].astype(F32)
                for s, (lo, hi) in enumerate(spans(chan)):
                    xs[b][s][pl.ds((start + y) * pitch + lead, side), 0 : hi - lo] = row[:, lo:hi]

        for y in range(side):
            row = feats[b][y].astype(F32)
            for s, (lo, hi) in enumerate(spans(chan)):
                xs[b][s][pl.ds((lead + y) * pitch + lead, side), 0 : hi - lo] = row[:, lo:hi]
        for ref, at, count, first, half in ((cl, right_at, lead, 0, 5), (cr, left_at, 2, lead + side, 1)):
            if b == 0:
                for i in range(count):
                    spot = at + (i if i < half else i - half) * TALL[0]
                    lane = 0 if i < half else 64
                    col = ref[spot : spot + TALL[0], lane : lane + 48].astype(F32)
                    x0[pl.ds(first + i, EXT[0], stride=pitch), 0:48] = col[: EXT[0]]
                at += half * TALL[0]
            else:
                for s, (lo, hi) in enumerate(spans(chan)):
                    for i in range(count):
                        col = ref[at : at + TALL[b], 0 : hi - lo].astype(F32)
                        xs[b][s][pl.ds(first + i, EXT[b], stride=pitch), 0 : hi - lo] = col[: EXT[b]]
                        at += TALL[b]
            if ref is cl:
                right_at = at
            else:
                left_at = at
        clear_edges(place, xs[b], pitch, EXT[b], EXT[b], lead, 2)
        return down_at, up_at, right_at, left_at

    ats = (0, 0, 0, 0)
    for b in range(4):
        ats = assemble(b, ats)

    def steps(rows, count, body):
        step = rows // count
        if count == 1:
            body(0, step)
            return

        @pl.loop(0, count)
        def _(i):
            body(pl.multiple_of(i * step, 16), step)

    def spread(planes, target, rows, count, chan):
        def body(p, step):
            for dx in range(3):
                for s, (lo, hi) in enumerate(spans(chan)):
                    piece = planes[s][pl.ds(p + dx, step), 0 : hi - lo].astype(BF)
                    target[pl.ds(p, step), dx * chan + lo : dx * chan + hi] = piece

        steps(rows, count, body)

    def block(b, weight, bias, source, counts):
        pitch, chan, lead = PITCH[b], CHAN[b], LEAD[b]
        width = 3 * chan

        def conv(i, p, step):
            total = None
            for dy in range(3):
                part = dot_nt(
                    source[pl.ds(p + dy * pitch, step), :],
                    weight[i, :, dy * width : (dy + 1) * width],
                )
                total = part if total is None else total + part
            return total + bias[i : i + 1, :]

        def inner(p, step):
            value = jnp.maximum(conv(0, p, step), 0.0)
            for s, (lo, hi) in enumerate(spans(chan)):
                hs[b][s][pl.ds(p, step), 0 : hi - lo] = value[:, lo:hi]

        def outer(p, step):
            total = conv(1, p, step)
            for s, (lo, hi) in enumerate(spans(chan)):
                kept = xs[b][s][pl.ds(p + 2 * pitch + 2, step), 0 : hi - lo]
                value = rounded(jnp.maximum(kept + total[:, lo:hi], 0.0))
                as_[b][s][pl.ds(p, step), 0 : hi - lo] = value

        inner_rows, outer_rows = (EXT[b] - 2) * pitch, (EXT[b] - 4) * pitch
        spread(xs[b], source, inner_rows + 2 * pitch, counts[0], chan)
        steps(inner_rows, counts[1], inner)
        clear_edges(place, hs[b], pitch, EXT[b] - 2, EXT[b] - 2, lead - 1, 1)
        spread(hs[b], source, outer_rows + 2 * pitch, counts[2], chan)
        steps(outer_rows, counts[3], outer)
        clear_edges(place, as_[b], pitch, EXT[b] - 4, EXT[b] - 4, lead - 2, 0)

    block(0, w0, b0, s0, (5, 5, 5, 5))
    copies[0].wait()
    block(1, w1, b1, s1, (3, 3, 3, 3))
    copies[1].wait()
    block(2, w2, b2, s2, (1, 2, 1, 2))
    copies[2].wait()
    block(3, w3, b3, s3, (1, 1, 1, 1))

    for copy in copies[3:]:
        copy.wait()
    d01[...] = jnp.zeros_like(d01)
    d01[0:96, :] = fin0[0:96, :]
    d01[128:176, :] = mid0[0]
    d01[192:240, :] = mid0[1]

    def halve(source, lane, chan, target, row, pitch, count):
        for dx in range(3):
            piece = source[pl.ds(row * pitch + dx, count, stride=2), :][:, lane : lane + chan]
            spot = pl.ds(row // 2 * count, count)
            target[row % 2, spot, dx * chan : (dx + 1) * chan] = piece.astype(BF)

    for row in range(71):
        halve(a0, 0, 48, t0, row, 80, 48)

    def first(p, step):
        total = None
        for dy in range(3):
            part = dot_nt(
                t0[dy % 2, pl.ds(p + (dy // 2) * 48, step), :], d01[:, dy * 144 : (dy + 1) * 144]
            )
            total = part if total is None else total + part
        v01[pl.ds(p, step), :] = rounded(total[:, :128])
        v0[pl.ds(p, step), :] = rounded(jnp.maximum(total[:, 128:], 0.0))

    steps(35 * 48, 5, first)
    clear_edges(place, [v0], 48, 35, 35, 3, 0)

    for row in range(35):
        halve(v0, 0, 48, ta, row, 48, 32)
        halve(v0, 64, 48, tb, row, 48, 32)
        halve(a1, 0, 96, t1, row, 48, 32)

    def second(source, p, n, weight):
        total = None
        for dy in range(3):
            part = dot_nt(source[dy % 2, p + dy // 2 * 32 : p + dy // 2 * 32 + n, :], weight(dy))
            total = part if total is None else total + part
        return total

    for p, n in ((0, 272), (272, 272)):
        cut = slice(p, p + n)
        total = rounded(second(ta, p, n, lambda dy: fin0[96:288, dy * 144 : (dy + 1) * 144]))
        vv02[0, cut, :] = total[:, :128]
        vv02[1, cut, 0:64] = total[:, 128:192]
        total = second(tb, p, n, lambda dy: mid0[2, :, dy * 144 : (dy + 1) * 144])
        n03[cut, :] = rounded(jnp.maximum(total, 0.0))
        total = rounded(second(t1, p, n, lambda dy: fin1[0:192, dy * 288 : (dy + 1) * 288]))
        vv12[0, cut, :] = total[:, :128]
        vv12[1, cut, 0:64] = total[:, 128:192]
        total = second(t1, p, n, lambda dy: mid1[:, dy * 288 : (dy + 1) * 288])
        m13[cut, :] = rounded(jnp.maximum(total, 0.0))

    clear_edges(place, [n03], 32, 17, 17, 1, 0)
    clear_edges(place, [m13], 32, 17, 17, 1, 0)

    def gathered(ref, width, dy, dx):
        return jnp.concatenate(
            [ref[pl.ds((2 * i + dy) * 32 + dx, 8, stride=2), 0:width] for i in range(8)], axis=0
        ).astype(BF)

    for tap in range(9):
        dy, dx = divmod(tap, 3)
        g03[:, tap * 48 : tap * 48 + 48] = gathered(n03, 48, dy, dx)
        g13[:, tap * 96 : tap * 96 + 96] = gathered(m13, 96, dy, dx)
        for s, (lo, hi) in enumerate(spans(192)):
            g23[:, tap * 192 + lo : tap * 192 + hi] = gathered(a2.at[s], hi - lo, dy, dx)
    t03 = dot_nt(g03[...], fin0[288:672, :])
    t13 = dot_nt(g13[...], fin1[192:576, :])
    t23 = jnp.dot(g23[...], fin2[...], preferred_element_type=F32)

    c3 = [
        jnp.concatenate([a3[s, y * 16 : y * 16 + 8, :] for y in range(8)], axis=0) for s in range(3)
    ]
    c3 = jnp.concatenate(c3, axis=1)
    three = jnp.maximum(c3 + rounded(t03) + rounded(t13) + rounded(t23), 0.0)
    j3[...] = three.reshape(8, 8, 384).astype(BF)

    c3b = c3.astype(BF)
    t30 = rounded(dot_nt(c3b, u3[0:48, :]))
    t31 = rounded(dot_nt(c3b, u3[48:144, :]))
    t32 = rounded(dot_nt(c3b, u3[144:336, :]))
    c2 = [
        jnp.concatenate([a2[s, pl.ds((y + 1) * 32 + 1, 16), 0 : hi - lo] for y in range(16)], axis=0)
        for s, (lo, hi) in enumerate(spans(192))
    ]
    c2 = jnp.concatenate(c2, axis=1)
    c2b = c2.astype(BF)
    t20 = rounded(dot_nt(c2b, u2[0:48, :]))
    t21 = rounded(dot_nt(c2b, u2[48:144, :]))

    def doubled(target, small, side, lanes):
        for y in range(side):
            row = small[y * side : (y + 1) * side]
            for odd in range(2):
                for right in range(2):
                    target[pl.ds((2 * y + odd) * 2 * side + right, side, stride=2), 0:lanes] = row

    for s, (lo, hi) in enumerate(spans(192)):
        doubled(wide, t32[:, lo:hi], 8, hi - lo)
        for y in range(16):
            t02 = vv02[s, pl.ds((y + 1) * 32 + 1, 16), 0 : hi - lo]
            t12 = vv12[s, pl.ds((y + 1) * 32 + 1, 16), 0 : hi - lo]
            keep = c2[y * 16 : (y + 1) * 16, lo:hi]
            row = keep + t02 + t12 + wide[pl.ds(y * 16, 16), 0 : hi - lo]
            j2[y, :, lo:hi] = jnp.maximum(row, 0.0).astype(BF)

    doubled(z2, t30, 8, 48)
    sum2 = z2[...] + t20
    doubled(z1, sum2, 16, 48)
    doubled(y2, t31, 8, 96)
    sum2 = y2[...] + t21
    doubled(y1, sum2, 16, 96)

    for y in range(32):
        c1[y * 32 : y * 32 + 32, :] = a1[pl.ds((y + 3) * 48 + 3, 32), 0:96].astype(BF)
    z1[...] += rounded(dot_nt(c1[...], u1[...]))

    @pl.loop(0, 8)
    def _(i):
        for y in range(4):
            y = 4 * i + y
            spot = pl.ds(pl.multiple_of(y * 32, 32), 32)
            one = a1[pl.ds((y + 3) * 48 + 3, 32), 0:96]
            t01 = v01[pl.ds((y + 3) * 48 + 3, 32), 0:96]
            j1[y] = jnp.maximum(one + t01 + y1[spot, :], 0.0).astype(BF)
            spread_row = mcol.at[y % 4]
            for right in range(2):
                spread_row[pl.ds(right, 32, stride=2), :] = z1[spot, :]
            pair = [
                jnp.maximum(a0[pl.ds((2 * y + odd + 7) * 80 + 7, 64), :] + spread_row[...], 0.0)
                for odd in range(2)
            ]
            turned = jnp.concatenate(pair, axis=0).T
            for odd in range(2):
                jt[pl.ds(2 * y + odd, 48, stride=64), :] = turned[:, odd * 64 : odd * 64 + 64]

    @pl.loop(0, 6)
    def _(i):
        for c in range(8):
            c = 8 * i + c
            j0[c] = jt[pl.ds(pl.multiple_of(c * 64, 64), 64), :].astype(BF)


def ring(x, axis, by):
    n = lax.axis_size(axis)
    return lax.ppermute(x, axis, [(i, (i + by) % n) for i in range(n)])


def shape(*dims, kind=BF):
    return jax.ShapeDtypeStruct(dims, kind)


def per_device(
    feat0, feat1, feat2, feat3,
    block_w0, block_w1, block_w2, block_w3,
    block_b0, block_b1, block_b2, block_b3,
    up_w1, up_w2, up_w3,
    down_mid0, down_mid1, down_fin0, down_fin1, down_fin2,
):
    maps = [f.transpose(1, 2, 0) for f in (feat0, feat1, feat2, feat3)]
    down, up = pl.pallas_call(
        pack_rows,
        out_shape=[shape(DOWN_ROWS, 128), shape(UP_ROWS, 128)],
        compiler_params=PARAMS,
    )(*maps)
    above, below = ring(down, "ty", 1), ring(up, "ty", -1)
    right, left = pl.pallas_call(
        pack_cols,
        out_shape=[shape(RIGHT_ROWS, 128), shape(LEFT_ROWS, 128)],
        scratch_shapes=[pltpu.VMEM((3, 80 * 16, 128), F32)],
        compiler_params=PARAMS,
    )(*maps, above, below)
    cl, cr = ring(right, "tx", 1), ring(left, "tx", -1)

    vmem = pl.BlockSpec(memory_space=pltpu.VMEM)
    f32 = lambda *dims: pltpu.VMEM(dims, F32)
    bf = lambda *dims: pltpu.VMEM(dims, BF)
    outs = pl.pallas_call(
        main,
        out_shape=[shape(48, 64, 64), shape(32, 32, 96), shape(16, 16, 192), shape(8, 8, 384)],
        in_specs=[vmem] * 14 + [pl.BlockSpec(memory_space=pltpu.HBM)] * 10,
        scratch_shapes=[
            bf(2, 96, 864), bf(2, 192, 1728), bf(2, 384, 3456), bf(3, 48, 432), bf(96, 864),
            bf(672, 432), bf(576, 864), bf(1728, 384), bf(336, 384), bf(144, 192),
            f32(6016, 48), f32(5856, 48), f32(5824, 48), bf(6000, 144), bf(2, 36 * 48, 144),
            bf(256, 432), f32(1728, 128), f32(1760, 128), bf(2, 18 * 32, 144), bf(2, 18 * 32, 144),
            f32(2, 544, 128), f32(544, 48), bf(64, 432),
            f32(1888, 96), f32(1792, 96), f32(1760, 96), bf(1872, 288), bf(2, 18 * 32, 288),
            f32(2, 544, 128), f32(544, 96), bf(64, 864),
            f32(2, 688, 128), f32(2, 624, 128), f32(2, 576, 128), bf(672, 576), bf(64, 1728),
            f32(3, 208, 128), f32(3, 176, 128), f32(3, 128, 128), bf(192, 1152),
            f32(1024, 48), f32(256, 48), f32(256, 96), f32(1024, 96), f32(256, 128),
            bf(1024, 96), f32(4, 64, 48), f32(3072, 64),
            pltpu.SemaphoreType.DMA((10,)),
        ],
        compiler_params=MAIN_PARAMS,
    )(
        *maps, above, below, cl, cr,
        block_w0, block_b0, block_b1, block_b2, block_b3, up_w1[0],
        block_w1, block_w2, block_w3, down_mid0[0], down_mid1[0, 0],
        down_fin0[0], down_fin1[0], down_fin2[0].T, up_w3[0], up_w2[0],
    )
    return (outs[0],) + tuple(o.transpose(2, 0, 1) for o in outs[1:])


def solution(mesh):
    tile = P(None, "ty", "tx")
    return jax.shard_map(
        per_device,
        mesh=mesh,
        in_specs=(tile,) * 4 + (P(),) * 16,
        out_specs=(tile,) * 4,
        check_vma=False,
    )
```

```python
import functools

import jax
import jax.numpy as jnp
from jax import lax
from jax.experimental import pallas as pl
from jax.experimental.pallas import tpu as pltpu
from jax.sharding import PartitionSpec as P

BF = jnp.bfloat16
F32 = jnp.float32
TILE = (64, 32, 16, 8)
CHAN = (48, 96, 192, 384)
LEAD = (9, 5, 3, 2)
EXT = (75, 39, 21, 12)
PITCH = (80, 48, 32, 16)
TALL = (80, 48, 32, 16)
GROUP = (16, 16, 16, 8)
DOWN_ROWS, UP_ROWS = 592, 240
RIGHT_ROWS, LEFT_ROWS = 928, 400
PARAMS = pltpu.CompilerParams(vmem_limit_bytes=16 * 2**20)
MAIN_PARAMS = pltpu.CompilerParams(vmem_limit_bytes=44 * 2**20)


def spans(chan):
    return [(lo, min(lo + 128, chan)) for lo in range(0, chan, 128)]


def put_packed(ref, at, value, branch, split):
    if branch == 0:
        ref[at : at + split, 0:48] = value[:split]
        ref[at : at + value.shape[0] - split, 64:112] = value[split:]
        return at + split
    for lo, hi in spans(CHAN[branch]):
        ref[at : at + value.shape[0], 0 : hi - lo] = value[:, lo:hi]
        at += value.shape[0]
    return at


def take_packed(ref, at, count, branch, split):
    if branch == 0:
        return jnp.concatenate(
            [ref[at : at + split, 0:48], ref[at : at + count - split, 64:112]], axis=0
        ), at + split
    parts = []
    for lo, hi in spans(CHAN[branch]):
        parts.append(ref[at : at + count, 0 : hi - lo])
        at += count
    return (parts[0] if len(parts) == 1 else jnp.concatenate(parts, axis=1)), at


def flat_rows(ref, lo, hi, branch):
    side = TILE[branch]
    value = ref[lo:hi].astype(F32)
    return value.reshape((hi - lo) * side, CHAN[branch]).astype(BF)


def pack_rows(f0, f1, f2, f3, down, up):
    at = 0
    for b, f in enumerate((f0, f1, f2, f3)):
        at = put_packed(down, at, flat_rows(f, TILE[b] - LEAD[b], TILE[b], b), b, 288)
    at = 0
    for b, f in enumerate((f0, f1, f2, f3)):
        at = put_packed(up, at, flat_rows(f, 0, 2, b), b, 64)


def pack_cols(f0, f1, f2, f3, above, below, right, left, work):
    down_at = up_at = right_at = left_at = 0
    for b, f in enumerate((f0, f1, f2, f3)):
        side, lead, chan, group = TILE[b], LEAD[b], CHAN[b], GROUP[b]
        high, down_at = take_packed(above, down_at, lead * side, b, 288)
        low, up_at = take_packed(below, up_at, 2 * side, b, 64)
        parts = (
            (high.astype(F32).reshape(lead, side, chan), 0, lead),
            (f[...].astype(F32).reshape(side, side, chan), lead, side),
            (low.astype(F32).reshape(2, side, chan), lead + side, 2),
        )
        for last in (True, False):
            cut = slice(side - group, side) if last else slice(0, group)
            for value, start, count in parts:
                edge = value[:, cut].reshape(count * group, chan)
                for s, (lo, hi) in enumerate(spans(chan)):
                    work[s, start * group : (start + count) * group, 0 : hi - lo] = edge[:, lo:hi]
            columns = range(group - lead, group) if last else range(2)
            cols = []
            for k in columns:
                planes = [
                    work[s, pl.ds(k, TALL[b], stride=group), 0 : hi - lo]
                    for s, (lo, hi) in enumerate(spans(chan))
                ]
                cols.append([p.astype(BF) for p in planes])
            target, at = (right, right_at) if last else (left, left_at)
            if b == 0:
                half = 5 if last else 1
                for i, (col,) in enumerate(cols):
                    place = at + (i if i < half else i - half) * TALL[0]
                    lane = 0 if i < half else 64
                    target[place : place + TALL[0], lane : lane + 48] = col
                at += half * TALL[0]
            else:
                for s, (lo, hi) in enumerate(spans(chan)):
                    for col in cols:
                        target[at : at + TALL[b], 0 : hi - lo] = col[s]
                        at += TALL[b]
            if last:
                right_at = at
            else:
                left_at = at


def clear_edges(place, planes, per, pitch, height, breadth, lead, trail):
    groups = -(-height // per)

    def rows(lo, count):
        for r in range(lo, lo + count):
            spot = slice(r // per * pitch, (r // per + 1) * pitch)
            if per == 4:
                lane = 64 * (r % 2)
                planes[r % 4 // 2][spot, lane : lane + 64] = jnp.zeros((pitch, 64), F32)
            else:
                for ref in [planes[r % 2]] if per == 2 else planes:
                    ref[spot, :] = jnp.zeros((pitch, ref.shape[1]), F32)

    def cols(lo, count):
        for ref in planes:
            for k in range(lo, lo + count):
                ref[pl.ds(k, groups, stride=pitch), :] = jnp.zeros((groups, ref.shape[1]), F32)

    if lead:
        pl.when(place[0] == 0)(lambda: rows(0, lead))
        pl.when(place[1] == 0)(lambda: cols(0, lead))
    if trail:
        pl.when(place[0] == 7)(lambda: rows(height - trail, trail))
        pl.when(place[1] == 7)(lambda: cols(breadth - trail, trail))


def prepare(w0, w1, b0, b1, mid0, mid1, fin0, fin1, q0, q1, c0, c1, d01, d02, d12):
    for out in (q0, q1, c0, c1):
        out[...] = jnp.zeros_like(out)
    for w, q, bias, c, chan, per, slot in ((w0, q0, b0, c0, 48, 4, 64), (w1, q1, b1, c1, 96, 2, 128)):
        for j in range(per):
            c[:, j * slot : j * slot + chan] = bias[...]
            for dy in range(3):
                more, r = divmod(j + dy, per)
                for dx in range(3):
                    lane = more * 768 + dx * 256 + r * slot
                    tap = (dy * 3 + dx) * chan
                    for i in range(2):
                        q[i, j * slot : j * slot + chan, lane : lane + chan] = w[i, :, tap : tap + chan]


    for out in (d01, d02, d12):
        out[...] = jnp.zeros_like(out)
    for tap in range(9):
        dy, dx = divmod(tap, 3)
        cut = slice(tap * 48, tap * 48 + 48)
        lane = dy // 2 * 384 + dx * 128 + dy % 2 * 64
        d01[0:96, lane : lane + 48] = fin0[0:96, cut]
        d01[128:176, lane : lane + 48] = mid0[0, :, cut]
        d01[192:240, lane : lane + 48] = mid0[1, :, cut]
        lane = dy * 384 + dx * 128
        d02[0:192, lane : lane + 48] = fin0[96:288, cut]
        d02[192:240, lane + 64 : lane + 112] = mid0[2, :, cut]
        cut = slice(tap * 96, tap * 96 + 96)
        d12[0:192, lane : lane + 96] = fin1[0:192, cut]
        d12[256:352, lane : lane + 96] = mid1[:, cut]


def dot_nt(x, w):
    return lax.dot_general(x, w, (((1,), (1,)), ((), ())), preferred_element_type=F32)


def rounded(x):
    return x.astype(BF).astype(F32)


PER = (4, 2, 1, 1)


def main(f0, f1, f2, f3, above, below, cl, cr, b0, b1, b2, b3, u1, *rest):
    ready, far, rest = rest[:5], rest[5:12], rest[12:]
    outs, near, scratch = rest[:4], rest[4:11], rest[11:-1]
    main_body(
        f0, f1, f2, f3, above, below, cl, cr, b0, b1, b2, b3, u1, ready, far, near, rest[-1], *outs, *scratch
    )


def main_body(
    f0, f1, f2, f3, above, below, cl, cr, b0, b1, b2, b3, u1, ready, far, near, sems,
    j0, j1, j2, j3,
    x0, h0, a0, s0, t0, v01, v0, ta, vv02, n03, g03,
    x1, h1, a1, s1, t1, vv12, m13, g13,
    x2, h2, a2, s2, g23,
    x3, h3, a3, s3,
    z1, z2, y2, y1, wide, c1, mcol, jt, col_in, col_out, zw,
):
    copies = [pltpu.make_async_copy(a, b, sems.at[i]) for i, (a, b) in enumerate(zip(far, near))]
    for copy in copies:
        copy.start()
    q0, q1, d01, d02, d12 = ready
    w2, w3, fin0, fin1, fin2, u3, u2 = near
    place = (lax.axis_index("ty"), lax.axis_index("tx"))
    feats = (f0, f1, f2, f3)
    two = lambda ref: [ref.at[0], ref.at[1]]
    three = lambda ref: [ref.at[i] for i in range(3)]
    xs = (two(x0), two(x1), two(x2), three(x3))
    hs = (two(h0), two(h1), two(h2), three(h3))
    as_ = (two(a0), two(a1), two(a2), three(a3))
    x0[...] = jnp.zeros_like(x0)
    x1[...] = jnp.zeros_like(x1)

    def put_row(b, r, row):
        side, lead, pitch = TILE[b], LEAD[b], PITCH[b]
        spot = pl.ds(r // PER[b] * pitch + lead, side)
        if b == 0:
            lane = 64 * (r % 2)
            x0[r % 4 // 2, spot, lane : lane + 48] = row
        elif b == 1:
            x1[r % 2, spot, 0:96] = row
        else:
            for s, (lo, hi) in enumerate(spans(CHAN[b])):
                xs[b][s][spot, 0 : hi - lo] = row[:, lo:hi]

    def assemble(b, ats):
        side, lead, chan, pitch = TILE[b], LEAD[b], CHAN[b], PITCH[b]
        down_at, up_at, right_at, left_at = ats
        high, down_at = take_packed(above, down_at, lead * side, b, 288)
        low, up_at = take_packed(below, up_at, 2 * side, b, 64)
        for value, start, count in ((high, 0, lead), (low, lead + side, 2)):
            for y in range(count):
                put_row(b, start + y, value[y * side : (y + 1) * side].astype(F32))
        for y in range(side):
            put_row(b, lead + y, feats[b][y].astype(F32))
        for ref, at, count, begin, half in ((cl, right_at, lead, 0, 5), (cr, left_at, 2, lead + side, 1)):
            if b == 0:
                for i in range(count):
                    spot = at + (i if i < half else i - half) * TALL[0]
                    lane = 0 if i < half else 64
                    col_in[...] = ref[spot : spot + TALL[0], lane : lane + 48].astype(F32)
                    for j in range(4):
                        n = (EXT[0] - j + 3) // 4
                        lane = 64 * (j % 2)
                        col_out[i % 2, j // 2, 0:n, lane : lane + 48] = col_in[pl.ds(j, n, stride=4), :]
                    for s in range(2):
                        x0[s, pl.ds(begin + i, 19, stride=pitch), :] = col_out[i % 2, s, 0:19, :]
                at += half * TALL[0]
            else:
                for s, (lo, hi) in enumerate(spans(chan)):
                    for i in range(count):
                        col = ref[at : at + TALL[b], 0 : hi - lo].astype(F32)
                        at += TALL[b]
                        if b == 1:
                            col_out[0, 0, 0 : TALL[1], 0:96] = col
                            for j in range(2):
                                n = (EXT[1] - j + 1) // 2
                                x1[j, pl.ds(begin + i, n, stride=pitch), :] = col_out[0, 0, pl.ds(j, n, stride=2), :]
                        else:
                            xs[b][s][pl.ds(begin + i, EXT[b], stride=pitch), 0 : hi - lo] = col[: EXT[b]]
            if ref is cl:
                right_at = at
            else:
                left_at = at
        clear_edges(place, xs[b], PER[b], pitch, EXT[b], EXT[b], lead, 2)
        return down_at, up_at, right_at, left_at

    col_out[...] = jnp.zeros_like(col_out)
    ats = (0, 0, 0, 0)
    for b in range(4):
        ats = assemble(b, ats)

    def steps(rows, count, body):
        step = rows // count
        if count == 1:
            body(0, step)
            return

        @pl.loop(0, count)
        def _(i):
            body(pl.multiple_of(i * step, 16), step)

    def spread(planes, target, rows, count, slot):
        def body(p, step):
            for dx in range(3):
                for s, plane in enumerate(planes):
                    piece = plane[pl.ds(p + dx, step), :].astype(BF)
                    target[pl.ds(p, step), dx * slot + s * 128 : dx * slot + s * 128 + 128] = piece

        steps(rows, count, body)

    def side_by_side(planes, target, rows):
        for tap in range(9):
            at = tap // 3 * 32 + tap % 3
            piece = jnp.concatenate(
                [planes[0][at : at + rows, :], planes[1][at : at + rows, 0:64]], axis=1
            )
            target[0:rows, tap * 192 : tap * 192 + 192] = piece.astype(BF)

    def block(b, weight, bias, source, counts):
        pitch, chan, lead, per = PITCH[b], CHAN[b], LEAD[b], PER[b]
        reach = (2, 2, 1, 3)[b]
        slot = 384 if b == 3 else 256

        def conv(i, p, step):
            taps = [source[pl.ds(p + k * pitch, step), :] for k in range(reach)]
            return dot_nt(jnp.concatenate(taps, axis=1), weight[i]) + bias[i : i + 1, :]

        def cuts(total):
            return [(s, lo, hi) for s, (lo, hi) in enumerate(spans(total.shape[1]))]

        def inner(p, step):
            value = jnp.maximum(conv(0, p, step), 0.0)
            for s, lo, hi in cuts(value):
                hs[b][s][pl.ds(p, step), 0 : hi - lo] = value[:, lo:hi]

        def outer(p, step):
            total = conv(1, p, step)
            for s, lo, hi in cuts(total):
                if per == 4:
                    kept = x0[1 - s, pl.ds(p + s * pitch + 2, step), :]
                elif per == 2:
                    kept = x1[s, pl.ds(p + pitch + 2, step), :]
                else:
                    kept = xs[b][s][pl.ds(p + 2 * pitch + 2, step), 0 : hi - lo]
                value = rounded(jnp.maximum(kept + total[:, lo:hi], 0.0))
                as_[b][s][pl.ds(p, step), 0 : hi - lo] = value

        inner_rows = -(-(EXT[b] - 2) // per) * pitch
        outer_rows = -(-(EXT[b] - 4) // per) * pitch
        extra = (reach - 1) * pitch
        if b == 2:
            side_by_side(xs[b], source, inner_rows)
        else:
            spread(xs[b], source, inner_rows + extra, counts[0], slot)
        steps(inner_rows, counts[1], inner)
        clear_edges(place, hs[b], per, pitch, EXT[b] - 2, EXT[b] - 2, lead - 1, 1)
        if b == 2:
            side_by_side(hs[b], source, outer_rows)
        else:
            spread(hs[b], source, outer_rows + extra, counts[2], slot)
        steps(outer_rows, counts[3], outer)
        clear_edges(place, as_[b], per, pitch, EXT[b] - 4, EXT[b] - 4, lead - 2, 0)

    block(0, q0, b0, s0, (5, 5, 5, 5))
    block(1, q1, b1, s1, (3, 3, 3, 3))
    copies[0].wait()
    block(2, w2, b2, s2, (1, 2, 1, 2))
    copies[1].wait()
    block(3, w3, b3, s3, (1, 1, 1, 1))
    for copy in copies[2:]:
        copy.wait()

    for pair in range(36):
        for dx in range(3):
            piece = a0[pair % 2, pl.ds(pair // 2 * 80 + dx, 48, stride=2), :]
            t0[pair * 48 : pair * 48 + 48, dx * 128 : dx * 128 + 128] = piece.astype(BF)

    def first(p, step):
        both = jnp.concatenate([t0[pl.ds(p, step), :], t0[pl.ds(p + 48, step), :]], axis=1)
        total = dot_nt(both, d01[...])
        v01[pl.ds(p, step), :] = rounded(total[:, :128])
        v0[pl.ds(p, step), :] = rounded(jnp.maximum(total[:, 128:], 0.0))

    steps(35 * 48, 5, first)
    clear_edges(place, [v0], 1, 48, 35, 35, 3, 0)

    for row in range(35):
        spot = slice(row // 2 * 32, row // 2 * 32 + 32)
        for dx in range(3):
            lane = slice(dx * 128, dx * 128 + 128)
            ta[row % 2, spot, lane] = v0[pl.ds(row * 48 + dx, 32, stride=2), :].astype(BF)
            piece = a1[row % 2, pl.ds(row // 2 * 48 + dx, 32, stride=2), :]
            t1[row % 2, spot, lane] = piece.astype(BF)

    def second(source, p, n, weight):
        taps = [source[dy % 2, p + dy // 2 * 32 : p + dy // 2 * 32 + n, :] for dy in range(3)]
        return dot_nt(jnp.concatenate(taps, axis=1), weight[...])

    for p, n in ((0, 272), (272, 272)):
        cut = slice(p, p + n)
        total = second(ta, p, n, d02)
        vv02[0, cut, :] = rounded(total[:, :128])
        vv02[1, cut, 0:64] = rounded(total[:, 128:192])
        n03[cut, :] = rounded(jnp.maximum(total[:, 192:240], 0.0))
        total = second(t1, p, n, d12)
        vv12[0, cut, :] = rounded(total[:, :128])
        vv12[1, cut, 0:64] = rounded(total[:, 128:192])
        m13[cut, :] = rounded(jnp.maximum(total[:, 256:352], 0.0))

    clear_edges(place, [n03], 1, 32, 17, 17, 1, 0)
    clear_edges(place, [m13], 1, 32, 17, 17, 1, 0)

    def gathered(ref, width, dy, dx):
        return jnp.concatenate(
            [ref[pl.ds((2 * i + dy) * 32 + dx, 8, stride=2), 0:width] for i in range(8)], axis=0
        ).astype(BF)

    for tap in range(9):
        dy, dx = divmod(tap, 3)
        g03[:, tap * 48 : tap * 48 + 48] = gathered(n03, 48, dy, dx)
        g13[:, tap * 96 : tap * 96 + 96] = gathered(m13, 96, dy, dx)
        for s, (lo, hi) in enumerate(spans(192)):
            g23[:, tap * 192 + lo : tap * 192 + hi] = gathered(a2.at[s], hi - lo, dy, dx)
    t03 = dot_nt(g03[...], fin0[288:672, :])
    t13 = dot_nt(g13[...], fin1[192:576, :])
    t23 = jnp.dot(g23[...], fin2[...], preferred_element_type=F32)

    c3 = [
        jnp.concatenate([a3[s, y * 16 : y * 16 + 8, :] for y in range(8)], axis=0) for s in range(3)
    ]
    c3 = jnp.concatenate(c3, axis=1)
    three = jnp.maximum(c3 + rounded(t03) + rounded(t13) + rounded(t23), 0.0)
    j3[...] = three.reshape(8, 8, 384).astype(BF)

    c3b = c3.astype(BF)
    t30 = rounded(dot_nt(c3b, u3[0:48, :]))
    t31 = rounded(dot_nt(c3b, u3[48:144, :]))
    t32 = rounded(dot_nt(c3b, u3[144:336, :]))
    c2 = [
        jnp.concatenate([a2[s, pl.ds((y + 1) * 32 + 1, 16), 0 : hi - lo] for y in range(16)], axis=0)
        for s, (lo, hi) in enumerate(spans(192))
    ]
    c2 = jnp.concatenate(c2, axis=1)
    c2b = c2.astype(BF)
    t20 = rounded(dot_nt(c2b, u2[0:48, :]))
    t21 = rounded(dot_nt(c2b, u2[48:144, :]))

    def doubled(target, small, side, lanes):
        for y in range(side):
            row = small[y * side : (y + 1) * side]
            for odd in range(2):
                for right in range(2):
                    target[pl.ds((2 * y + odd) * 2 * side + right, side, stride=2), 0:lanes] = row

    for s, (lo, hi) in enumerate(spans(192)):
        doubled(wide, t32[:, lo:hi], 8, hi - lo)
        for y in range(16):
            t02 = vv02[s, pl.ds((y + 1) * 32 + 1, 16), 0 : hi - lo]
            t12 = vv12[s, pl.ds((y + 1) * 32 + 1, 16), 0 : hi - lo]
            keep = c2[y * 16 : (y + 1) * 16, lo:hi]
            row = keep + t02 + t12 + wide[pl.ds(y * 16, 16), 0 : hi - lo]
            j2[y, :, lo:hi] = jnp.maximum(row, 0.0).astype(BF)

    doubled(z2, t30, 8, 48)
    sum2 = z2[...] + t20
    doubled(z1, sum2, 16, 48)
    doubled(y2, t31, 8, 96)
    sum2 = y2[...] + t21
    doubled(y1, sum2, 16, 96)

    for y in range(32):
        row = a1[(y + 3) % 2, pl.ds((y + 3) // 2 * 48 + 3, 32), 0:96]
        c1[y * 32 : y * 32 + 32, :] = row.astype(BF)
    total = z1[...] + rounded(dot_nt(c1[...], u1[...]))
    zw[32:1056, 0:48] = total
    zw[0:1024, 64:112] = total

    def last_rows(m, plane, group, k):
        for right in range(2):
            mcol[k, pl.ds(right, 32, stride=2), :] = zw[pl.ds(m * 32, 32), :]
        zero = a0[plane, pl.ds(group * 80 + 7, 64), :]
        turned = jnp.maximum(zero + mcol[k], 0.0).T
        jt[pl.ds(2 * m + 7, 48, stride=80), :] = turned[0:48]
        jt[pl.ds(2 * m + 8, 48, stride=80), :] = turned[64:112]

    @pl.loop(0, 8)
    def _(i):
        for k in range(4):
            y = 4 * i + k
            spot = pl.ds(pl.multiple_of(y * 32, 32), 32)
            one = a1[(k + 3) % 2, pl.ds((2 * i + (k + 3) // 2) * 48 + 3, 32), 0:96]
            t01 = v01[pl.ds((y + 3) * 48 + 3, 32), 0:96]
            j1[y] = jnp.maximum(one + t01 + y1[spot, :], 0.0).astype(BF)
            last_rows(y, (3 + k) % 2, 2 * i + (3 + k) // 2, k)

    last_rows(32, 1, 17, 0)

    @pl.loop(0, 6)
    def _(i):
        for c in range(8):
            c = 8 * i + c
            j0[c] = jt[pl.ds(pl.multiple_of(c * 80 + 8, 8), 64), :].astype(BF)


def ring(x, axis, by):
    n = lax.axis_size(axis)
    return lax.ppermute(x, axis, [(i, (i + by) % n) for i in range(n)])


def shape(*dims, kind=BF):
    return jax.ShapeDtypeStruct(dims, kind)


def per_device(
    feat0, feat1, feat2, feat3,
    block_w0, block_w1, block_w2, block_w3,
    block_b0, block_b1, block_b2, block_b3,
    up_w1, up_w2, up_w3,
    down_mid0, down_mid1, down_fin0, down_fin1, down_fin2,
):
    maps = [f.transpose(1, 2, 0) for f in (feat0, feat1, feat2, feat3)]
    down, up = pl.pallas_call(
        pack_rows,
        out_shape=[shape(DOWN_ROWS, 128), shape(UP_ROWS, 128)],
        compiler_params=PARAMS,
    )(*maps)
    above, below = ring(down, "ty", 1), ring(up, "ty", -1)
    fin0, fin1, mid0, mid1 = down_fin0[0], down_fin1[0], down_mid0[0], down_mid1[0, 0]
    above, below, fin0 = lax.optimization_barrier((above, below, fin0))
    right, left = pl.pallas_call(
        pack_cols,
        out_shape=[shape(RIGHT_ROWS, 128), shape(LEFT_ROWS, 128)],
        scratch_shapes=[pltpu.VMEM((3, 80 * 16, 128), F32)],
        compiler_params=PARAMS,
    )(*maps, above, below)
    cl, cr = ring(right, "tx", 1), ring(left, "tx", -1)

    q0, q1, c0, c1, d01, d02, d12 = pl.pallas_call(
        prepare,
        out_shape=[
            shape(2, 256, 1536), shape(2, 256, 1536), shape(2, 256, kind=F32), shape(2, 256, kind=F32),
            shape(256, 768), shape(256, 1152), shape(352, 1152),
        ],
        compiler_params=PARAMS,
    )(block_w0, block_w1, block_b0, block_b1, mid0, mid1, fin0, fin1)

    vmem = pl.BlockSpec(memory_space=pltpu.VMEM)
    f32 = lambda *dims: pltpu.VMEM(dims, F32)
    bf = lambda *dims: pltpu.VMEM(dims, BF)
    ready = (q0, q1, d01, d02, d12)
    far = (block_w2, block_w3, fin0, fin1, down_fin2[0].T, up_w3[0], up_w2[0])
    outs = pl.pallas_call(
        main,
        out_shape=[shape(48, 64, 64), shape(32, 32, 96), shape(16, 16, 192), shape(8, 8, 384)],
        in_specs=[vmem] * 18 + [pl.BlockSpec(memory_space=pltpu.HBM)] * 7,
        scratch_shapes=[bf(*w.shape) for w in far]
        + [
            f32(2, 1616, 128), f32(2, 1536, 128), f32(2, 1536, 128), bf(1600, 768), bf(1728, 384),
            f32(1728, 128), f32(1760, 128), bf(2, 18 * 32, 384), f32(2, 544, 128), f32(544, 48), bf(64, 432),
            f32(2, 976, 128), f32(2, 928, 128), f32(2, 896, 128), bf(960, 768), bf(2, 18 * 32, 384),
            f32(2, 544, 128), f32(544, 96), bf(64, 864),
            f32(2, 688, 128), f32(2, 624, 128), f32(2, 576, 128), bf(608, 1728), bf(64, 1728),
            f32(3, 208, 128), f32(3, 176, 128), f32(3, 128, 128), bf(192, 1152),
            f32(1024, 48), f32(256, 48), f32(256, 96), f32(1024, 96), f32(256, 128),
            bf(1024, 96), f32(4, 64, 128), f32(3840, 64), f32(80, 48), f32(2, 2, 48, 128), f32(1056, 128),
            pltpu.SemaphoreType.DMA((7,)),
        ],
        compiler_params=MAIN_PARAMS,
    )(*maps, above, below, cl, cr, c0, c1, block_b2, block_b3, up_w1[0], *ready, *far)
    return (outs[0],) + tuple(o.transpose(2, 0, 1) for o in outs[1:])


def solution(mesh):
    tile = P(None, "ty", "tx")
    return jax.shard_map(
        per_device,
        mesh=mesh,
        in_specs=(tile,) * 4 + (P(),) * 16,
        out_specs=(tile,) * 4,
        check_vma=False,
    )
```

```python
import functools

import jax
import jax.numpy as jnp
from jax import lax
from jax.experimental import pallas as pl
from jax.experimental.pallas import tpu as pltpu
from jax.sharding import PartitionSpec as P

BF = jnp.bfloat16
F32 = jnp.float32
TILE = (64, 32, 16, 8)
CHAN = (48, 96, 192, 384)
LEAD = (9, 5, 3, 2)
EXT = (75, 39, 21, 12)
PITCH = (80, 48, 32, 16)
TALL = (80, 48, 32, 16)
GROUP = (16, 16, 16, 8)
DOWN_ROWS, UP_ROWS = 592, 240
RIGHT_ROWS, LEFT_ROWS = 928, 400
PARAMS = pltpu.CompilerParams(vmem_limit_bytes=16 * 2**20)
MAIN_PARAMS = pltpu.CompilerParams(vmem_limit_bytes=39 * 2**20)


def spans(chan):
    return [(lo, min(lo + 128, chan)) for lo in range(0, chan, 128)]


def put_packed(ref, at, value, branch, split):
    if branch == 0:
        ref[at : at + split, 0:48] = value[:split]
        ref[at : at + value.shape[0] - split, 64:112] = value[split:]
        return at + split
    for lo, hi in spans(CHAN[branch]):
        ref[at : at + value.shape[0], 0 : hi - lo] = value[:, lo:hi]
        at += value.shape[0]
    return at


def take_packed(ref, at, count, branch, split):
    if branch == 0:
        return jnp.concatenate(
            [ref[at : at + split, 0:48], ref[at : at + count - split, 64:112]], axis=0
        ), at + split
    parts = []
    for lo, hi in spans(CHAN[branch]):
        parts.append(ref[at : at + count, 0 : hi - lo])
        at += count
    return (parts[0] if len(parts) == 1 else jnp.concatenate(parts, axis=1)), at


def flat_rows(ref, lo, hi, branch):
    side = TILE[branch]
    value = ref[lo:hi].astype(F32)
    return value.reshape((hi - lo) * side, CHAN[branch]).astype(BF)


def pack_rows(f0, f1, f2, f3, down, up):
    at = 0
    for b, f in enumerate((f0, f1, f2, f3)):
        at = put_packed(down, at, flat_rows(f, TILE[b] - LEAD[b], TILE[b], b), b, 288)
    at = 0
    for b, f in enumerate((f0, f1, f2, f3)):
        at = put_packed(up, at, flat_rows(f, 0, 2, b), b, 64)


def pack_cols(f0, f1, f2, f3, above, below, right, left, work):
    down_at = up_at = right_at = left_at = 0
    for b, f in enumerate((f0, f1, f2, f3)):
        side, lead, chan, group = TILE[b], LEAD[b], CHAN[b], GROUP[b]
        high, down_at = take_packed(above, down_at, lead * side, b, 288)
        low, up_at = take_packed(below, up_at, 2 * side, b, 64)
        parts = (
            (high.astype(F32).reshape(lead, side, chan), 0, lead),
            (f[...].astype(F32).reshape(side, side, chan), lead, side),
            (low.astype(F32).reshape(2, side, chan), lead + side, 2),
        )
        for last in (True, False):
            cut = slice(side - group, side) if last else slice(0, group)
            for value, start, count in parts:
                edge = value[:, cut].reshape(count * group, chan)
                for s, (lo, hi) in enumerate(spans(chan)):
                    work[s, start * group : (start + count) * group, 0 : hi - lo] = edge[:, lo:hi]
            columns = range(group - lead, group) if last else range(2)
            cols = []
            for k in columns:
                planes = [
                    work[s, pl.ds(k, TALL[b], stride=group), 0 : hi - lo]
                    for s, (lo, hi) in enumerate(spans(chan))
                ]
                cols.append([p.astype(BF) for p in planes])
            target, at = (right, right_at) if last else (left, left_at)
            if b == 0:
                half = 5 if last else 1
                for i, (col,) in enumerate(cols):
                    place = at + (i if i < half else i - half) * TALL[0]
                    lane = 0 if i < half else 64
                    target[place : place + TALL[0], lane : lane + 48] = col
                at += half * TALL[0]
            else:
                for s, (lo, hi) in enumerate(spans(chan)):
                    for col in cols:
                        target[at : at + TALL[b], 0 : hi - lo] = col[s]
                        at += TALL[b]
            if last:
                right_at = at
            else:
                left_at = at


def clear_edges(place, planes, per, pitch, height, breadth, lead, trail):
    groups = -(-height // per)

    def rows(lo, count):
        for r in range(lo, lo + count):
            spot = slice(r // per * pitch, (r // per + 1) * pitch)
            if per == 4:
                lane = 64 * (r % 2)
                planes[r % 4 // 2][spot, lane : lane + 64] = jnp.zeros((pitch, 64), F32)
            else:
                for ref in [planes[r % 2]] if per == 2 else planes:
                    ref[spot, :] = jnp.zeros((pitch, ref.shape[1]), F32)

    def cols(lo, count):
        for ref in planes:
            for k in range(lo, lo + count):
                ref[pl.ds(k, groups, stride=pitch), :] = jnp.zeros((groups, ref.shape[1]), F32)

    if lead:
        pl.when(place[0] == 0)(lambda: rows(0, lead))
        pl.when(place[1] == 0)(lambda: cols(0, lead))
    if trail:
        pl.when(place[0] == 7)(lambda: rows(height - trail, trail))
        pl.when(place[1] == 7)(lambda: cols(breadth - trail, trail))


def prepare(w0, w1, b0, b1, mid0, mid1, fin0, fin1, q0, q1, c0, c1, d01, d02, d12):
    for out in (q0, q1, c0, c1):
        out[...] = jnp.zeros_like(out)
    for w, q, bias, c, chan, per, slot in ((w0, q0, b0, c0, 48, 4, 64), (w1, q1, b1, c1, 96, 2, 128)):
        for j in range(per):
            c[:, j * slot : j * slot + chan] = bias[...]
            for dy in range(3):
                more, r = divmod(j + dy, per)
                for dx in range(3):
                    lane = more * 768 + dx * 256 + r * slot
                    tap = (dy * 3 + dx) * chan
                    for i in range(2):
                        q[i, j * slot : j * slot + chan, lane : lane + chan] = w[i, :, tap : tap + chan]


    for out in (d01, d02, d12):
        out[...] = jnp.zeros_like(out)
    for tap in range(9):
        dy, dx = divmod(tap, 3)
        cut = slice(tap * 48, tap * 48 + 48)
        lane = dy // 2 * 384 + dx * 128 + dy % 2 * 64
        d01[0:96, lane : lane + 48] = fin0[0:96, cut]
        d01[128:176, lane : lane + 48] = mid0[0, :, cut]
        d01[192:240, lane : lane + 48] = mid0[1, :, cut]
        lane = dy * 384 + dx * 128
        d02[0:192, lane : lane + 48] = fin0[96:288, cut]
        d02[192:240, lane + 64 : lane + 112] = mid0[2, :, cut]
        cut = slice(tap * 96, tap * 96 + 96)
        d12[0:192, lane : lane + 96] = fin1[0:192, cut]
        d12[256:352, lane : lane + 96] = mid1[:, cut]


def dot_nt(x, w):
    return lax.dot_general(x, w, (((1,), (1,)), ((), ())), preferred_element_type=F32)


def rounded(x):
    return x.astype(BF).astype(F32)


PER = (4, 2, 1, 1)


def main(f0, f1, f2, f3, above, below, cl, cr, b0, b1, b2, b3, u1, *rest):
    ready, far, rest = rest[:11], rest[11:12], rest[12:]
    outs, near, scratch = rest[:4], rest[4:5], rest[5:-1]
    main_body(
        f0, f1, f2, f3, above, below, cl, cr, b0, b1, b2, b3, u1, ready, far, near, rest[-1], *outs, *scratch
    )


def main_body(
    f0, f1, f2, f3, above, below, cl, cr, b0, b1, b2, b3, u1, ready, far, near, sems,
    j0, j1, j2, j3,
    x0, h0, a0, s0, t0, v01, v0, ta, vv02, n03, g03,
    x1, h1, a1, s1, t1, vv12, m13, g13,
    x2, h2, a2, s2, g23,
    x3, h3, a3, s3,
    z1, z2, y2, y1, wide, c1, mcol, jt, col_in, col_out, zw,
):
    copies = [pltpu.make_async_copy(a, b, sems.at[i]) for i, (a, b) in enumerate(zip(far, near))]
    for copy in copies:
        copy.start()
    q0, q1, d01, d02, d12, fin0, fin1, fin2, u3, u2, w2 = ready
    w3 = near[0]
    place = (lax.axis_index("ty"), lax.axis_index("tx"))
    feats = (f0, f1, f2, f3)
    two = lambda ref: [ref.at[0], ref.at[1]]
    three = lambda ref: [ref.at[i] for i in range(3)]
    xs = (two(x0), two(x1), two(x2), three(x3))
    hs = (two(h0), two(h1), two(h2), three(h3))
    as_ = (two(a0), two(a1), two(a2), three(a3))
    x0[...] = jnp.zeros_like(x0)
    x1[...] = jnp.zeros_like(x1)

    def put_row(b, r, row):
        side, lead, pitch = TILE[b], LEAD[b], PITCH[b]
        spot = pl.ds(r // PER[b] * pitch + lead, side)
        if b == 0:
            lane = 64 * (r % 2)
            x0[r % 4 // 2, spot, lane : lane + 48] = row
        elif b == 1:
            x1[r % 2, spot, 0:96] = row
        else:
            for s, (lo, hi) in enumerate(spans(CHAN[b])):
                xs[b][s][spot, 0 : hi - lo] = row[:, lo:hi]

    def assemble(b, ats):
        side, lead, chan, pitch = TILE[b], LEAD[b], CHAN[b], PITCH[b]
        down_at, up_at, right_at, left_at = ats
        high, down_at = take_packed(above, down_at, lead * side, b, 288)
        low, up_at = take_packed(below, up_at, 2 * side, b, 64)
        for value, start, count in ((high, 0, lead), (low, lead + side, 2)):
            for y in range(count):
                put_row(b, start + y, value[y * side : (y + 1) * side].astype(F32))
        for y in range(side):
            put_row(b, lead + y, feats[b][y].astype(F32))
        for ref, at, count, begin, half in ((cl, right_at, lead, 0, 5), (cr, left_at, 2, lead + side, 1)):
            if b == 0:
                for i in range(count):
                    spot = at + (i if i < half else i - half) * TALL[0]
                    lane = 0 if i < half else 64
                    col_in[...] = ref[spot : spot + TALL[0], lane : lane + 48].astype(F32)
                    for j in range(4):
                        n = (EXT[0] - j + 3) // 4
                        lane = 64 * (j % 2)
                        col_out[i % 2, j // 2, 0:n, lane : lane + 48] = col_in[pl.ds(j, n, stride=4), :]
                    for s in range(2):
                        x0[s, pl.ds(begin + i, 19, stride=pitch), :] = col_out[i % 2, s, 0:19, :]
                at += half * TALL[0]
            else:
                for s, (lo, hi) in enumerate(spans(chan)):
                    for i in range(count):
                        col = ref[at : at + TALL[b], 0 : hi - lo].astype(F32)
                        at += TALL[b]
                        if b == 1:
                            col_out[0, 0, 0 : TALL[1], 0:96] = col
                            for j in range(2):
                                n = (EXT[1] - j + 1) // 2
                                x1[j, pl.ds(begin + i, n, stride=pitch), :] = col_out[0, 0, pl.ds(j, n, stride=2), :]
                        else:
                            xs[b][s][pl.ds(begin + i, EXT[b], stride=pitch), 0 : hi - lo] = col[: EXT[b]]
            if ref is cl:
                right_at = at
            else:
                left_at = at
        clear_edges(place, xs[b], PER[b], pitch, EXT[b], EXT[b], lead, 2)
        return down_at, up_at, right_at, left_at

    col_out[...] = jnp.zeros_like(col_out)
    ats = (0, 0, 0, 0)
    for b in range(4):
        ats = assemble(b, ats)

    def steps(rows, count, body):
        step = rows // count
        if count == 1:
            body(0, step)
            return

        @pl.loop(0, count)
        def _(i):
            body(pl.multiple_of(i * step, 16), step)

    def spread(planes, target, rows, count, slot):
        def body(p, step):
            for dx in range(3):
                for s, plane in enumerate(planes):
                    piece = plane[pl.ds(p + dx, step), :].astype(BF)
                    target[pl.ds(p, step), dx * slot + s * 128 : dx * slot + s * 128 + 128] = piece

        steps(rows, count, body)

    def side_by_side(planes, target, rows):
        for tap in range(9):
            at = tap // 3 * 32 + tap % 3
            piece = jnp.concatenate(
                [planes[0][at : at + rows, :], planes[1][at : at + rows, 0:64]], axis=1
            )
            target[0:rows, tap * 192 : tap * 192 + 192] = piece.astype(BF)

    def block(b, weight, bias, source, counts):
        pitch, chan, lead, per = PITCH[b], CHAN[b], LEAD[b], PER[b]
        reach = (2, 2, 1, 3)[b]
        slot = 384 if b == 3 else 256

        def conv(i, p, step):
            taps = [source[pl.ds(p + k * pitch, step), :] for k in range(reach)]
            return dot_nt(jnp.concatenate(taps, axis=1), weight[i]) + bias[i : i + 1, :]

        def cuts(total):
            return [(s, lo, hi) for s, (lo, hi) in enumerate(spans(total.shape[1]))]

        def inner(p, step):
            value = jnp.maximum(conv(0, p, step), 0.0)
            for s, lo, hi in cuts(value):
                hs[b][s][pl.ds(p, step), 0 : hi - lo] = value[:, lo:hi]

        def outer(p, step):
            total = conv(1, p, step)
            for s, lo, hi in cuts(total):
                if per == 4:
                    kept = x0[1 - s, pl.ds(p + s * pitch + 2, step), :]
                elif per == 2:
                    kept = x1[s, pl.ds(p + pitch + 2, step), :]
                else:
                    kept = xs[b][s][pl.ds(p + 2 * pitch + 2, step), 0 : hi - lo]
                value = rounded(jnp.maximum(kept + total[:, lo:hi], 0.0))
                as_[b][s][pl.ds(p, step), 0 : hi - lo] = value

        inner_rows = -(-(EXT[b] - 2) // per) * pitch
        outer_rows = -(-(EXT[b] - 4) // per) * pitch
        extra = (reach - 1) * pitch
        if b == 2:
            side_by_side(xs[b], source, inner_rows)
        else:
            spread(xs[b], source, inner_rows + extra, counts[0], slot)
        steps(inner_rows, counts[1], inner)
        clear_edges(place, hs[b], per, pitch, EXT[b] - 2, EXT[b] - 2, lead - 1, 1)
        if b == 2:
            side_by_side(hs[b], source, outer_rows)
        else:
            spread(hs[b], source, outer_rows + extra, counts[2], slot)
        steps(outer_rows, counts[3], outer)
        clear_edges(place, as_[b], per, pitch, EXT[b] - 4, EXT[b] - 4, lead - 2, 0)

    block(0, q0, b0, s0, (1, 1, 1, 1))
    block(1, q1, b1, s1, (1, 1, 1, 1))
    block(2, w2, b2, s2, (1, 1, 1, 1))
    copies[0].wait()
    block(3, w3, b3, s3, (1, 1, 1, 1))

    for pair in range(36):
        for dx in range(3):
            piece = a0[pair % 2, pl.ds(pair // 2 * 80 + dx, 48, stride=2), :]
            t0[pair * 48 : pair * 48 + 48, dx * 128 : dx * 128 + 128] = piece.astype(BF)

    def first(p, step):
        both = jnp.concatenate([t0[pl.ds(p, step), :], t0[pl.ds(p + 48, step), :]], axis=1)
        total = dot_nt(both, d01[...])
        v01[pl.ds(p, step), :] = rounded(total[:, :128])
        v0[pl.ds(p, step), :] = rounded(jnp.maximum(total[:, 128:], 0.0))

    steps(35 * 48, 5, first)
    clear_edges(place, [v0], 1, 48, 35, 35, 3, 0)

    for row in range(35):
        spot = slice(row // 2 * 32, row // 2 * 32 + 32)
        for dx in range(3):
            lane = slice(dx * 128, dx * 128 + 128)
            ta[row % 2, spot, lane] = v0[pl.ds(row * 48 + dx, 32, stride=2), :].astype(BF)
            piece = a1[row % 2, pl.ds(row // 2 * 48 + dx, 32, stride=2), :]
            t1[row % 2, spot, lane] = piece.astype(BF)

    def second(source, p, n, weight):
        taps = [source[dy % 2, p + dy // 2 * 32 : p + dy // 2 * 32 + n, :] for dy in range(3)]
        return dot_nt(jnp.concatenate(taps, axis=1), weight[...])

    for p, n in ((0, 272), (272, 272)):
        cut = slice(p, p + n)
        total = second(ta, p, n, d02)
        vv02[0, cut, :] = rounded(total[:, :128])
        vv02[1, cut, 0:64] = rounded(total[:, 128:192])
        n03[cut, :] = rounded(jnp.maximum(total[:, 192:240], 0.0))
        total = second(t1, p, n, d12)
        vv12[0, cut, :] = rounded(total[:, :128])
        vv12[1, cut, 0:64] = rounded(total[:, 128:192])
        m13[cut, :] = rounded(jnp.maximum(total[:, 256:352], 0.0))

    clear_edges(place, [n03], 1, 32, 17, 17, 1, 0)
    clear_edges(place, [m13], 1, 32, 17, 17, 1, 0)

    def gathered(ref, width, dy, dx):
        return jnp.concatenate(
            [ref[pl.ds((2 * i + dy) * 32 + dx, 8, stride=2), 0:width] for i in range(8)], axis=0
        ).astype(BF)

    for tap in range(9):
        dy, dx = divmod(tap, 3)
        g03[:, tap * 48 : tap * 48 + 48] = gathered(n03, 48, dy, dx)
        g13[:, tap * 96 : tap * 96 + 96] = gathered(m13, 96, dy, dx)
        for s, (lo, hi) in enumerate(spans(192)):
            g23[:, tap * 192 + lo : tap * 192 + hi] = gathered(a2.at[s], hi - lo, dy, dx)
    t03 = dot_nt(g03[...], fin0[288:672, :])
    t13 = dot_nt(g13[...], fin1[192:576, :])
    t23 = jnp.dot(g23[...], fin2[...], preferred_element_type=F32)

    c3 = [
        jnp.concatenate([a3[s, y * 16 : y * 16 + 8, :] for y in range(8)], axis=0) for s in range(3)
    ]
    c3 = jnp.concatenate(c3, axis=1)
    three = jnp.maximum(c3 + rounded(t03) + rounded(t13) + rounded(t23), 0.0)
    j3[...] = three.reshape(8, 8, 384).astype(BF)

    c3b = c3.astype(BF)
    t30 = rounded(dot_nt(c3b, u3[0:48, :]))
    t31 = rounded(dot_nt(c3b, u3[48:144, :]))
    t32 = rounded(dot_nt(c3b, u3[144:336, :]))
    c2 = [
        jnp.concatenate([a2[s, pl.ds((y + 1) * 32 + 1, 16), 0 : hi - lo] for y in range(16)], axis=0)
        for s, (lo, hi) in enumerate(spans(192))
    ]
    c2 = jnp.concatenate(c2, axis=1)
    c2b = c2.astype(BF)
    t20 = rounded(dot_nt(c2b, u2[0:48, :]))
    t21 = rounded(dot_nt(c2b, u2[48:144, :]))

    def doubled(target, small, side, lanes):
        for y in range(side):
            row = small[y * side : (y + 1) * side]
            for odd in range(2):
                for right in range(2):
                    target[pl.ds((2 * y + odd) * 2 * side + right, side, stride=2), 0:lanes] = row

    for s, (lo, hi) in enumerate(spans(192)):
        doubled(wide, t32[:, lo:hi], 8, hi - lo)
        for y in range(16):
            t02 = vv02[s, pl.ds((y + 1) * 32 + 1, 16), 0 : hi - lo]
            t12 = vv12[s, pl.ds((y + 1) * 32 + 1, 16), 0 : hi - lo]
            keep = c2[y * 16 : (y + 1) * 16, lo:hi]
            row = keep + t02 + t12 + wide[pl.ds(y * 16, 16), 0 : hi - lo]
            j2[y, :, lo:hi] = jnp.maximum(row, 0.0).astype(BF)

    doubled(z2, t30, 8, 48)
    sum2 = z2[...] + t20
    doubled(z1, sum2, 16, 48)
    doubled(y2, t31, 8, 96)
    sum2 = y2[...] + t21
    doubled(y1, sum2, 16, 96)

    for y in range(32):
        row = a1[(y + 3) % 2, pl.ds((y + 3) // 2 * 48 + 3, 32), 0:96]
        c1[y * 32 : y * 32 + 32, :] = row.astype(BF)
    total = z1[...] + rounded(dot_nt(c1[...], u1[...]))
    zw[32:1056, 0:48] = total
    zw[0:1024, 64:112] = total

    def last_rows(m, plane, group, k):
        for right in range(2):
            mcol[k, pl.ds(right, 32, stride=2), :] = zw[pl.ds(m * 32, 32), :]
        zero = a0[plane, pl.ds(group * 80 + 7, 64), :]
        turned = jnp.maximum(zero + mcol[k], 0.0).T
        jt[pl.ds(2 * m + 7, 48, stride=80), :] = turned[0:48]
        jt[pl.ds(2 * m + 8, 48, stride=80), :] = turned[64:112]

    @pl.loop(0, 8)
    def _(i):
        for k in range(4):
            y = 4 * i + k
            spot = pl.ds(pl.multiple_of(y * 32, 32), 32)
            one = a1[(k + 3) % 2, pl.ds((2 * i + (k + 3) // 2) * 48 + 3, 32), 0:96]
            t01 = v01[pl.ds((y + 3) * 48 + 3, 32), 0:96]
            j1[y] = jnp.maximum(one + t01 + y1[spot, :], 0.0).astype(BF)
            last_rows(y, (3 + k) % 2, 2 * i + (3 + k) // 2, k)

    last_rows(32, 1, 17, 0)

    @pl.loop(0, 6)
    def _(i):
        for c in range(8):
            c = 8 * i + c
            j0[c] = jt[pl.ds(pl.multiple_of(c * 80 + 8, 8), 64), :].astype(BF)


def ring(x, axis, by):
    n = lax.axis_size(axis)
    return lax.ppermute(x, axis, [(i, (i + by) % n) for i in range(n)])


def shape(*dims, kind=BF):
    return jax.ShapeDtypeStruct(dims, kind)


def per_device(
    feat0, feat1, feat2, feat3,
    block_w0, block_w1, block_w2, block_w3,
    block_b0, block_b1, block_b2, block_b3,
    up_w1, up_w2, up_w3,
    down_mid0, down_mid1, down_fin0, down_fin1, down_fin2,
):
    maps = [f.transpose(1, 2, 0) for f in (feat0, feat1, feat2, feat3)]
    down, up = pl.pallas_call(
        pack_rows,
        out_shape=[shape(DOWN_ROWS, 128), shape(UP_ROWS, 128)],
        compiler_params=PARAMS,
    )(*maps)
    above, below = ring(down, "ty", 1), ring(up, "ty", -1)
    fin0, fin1, mid0, mid1 = down_fin0[0], down_fin1[0], down_mid0[0], down_mid1[0, 0]
    above, below, fin0 = lax.optimization_barrier((above, below, fin0))
    right, left = pl.pallas_call(
        pack_cols,
        out_shape=[shape(RIGHT_ROWS, 128), shape(LEFT_ROWS, 128)],
        scratch_shapes=[pltpu.VMEM((3, 80 * 16, 128), F32)],
        compiler_params=PARAMS,
    )(*maps, above, below)
    cl, cr = ring(right, "tx", 1), ring(left, "tx", -1)

    q0, q1, c0, c1, d01, d02, d12 = pl.pallas_call(
        prepare,
        out_shape=[
            shape(2, 256, 1536), shape(2, 256, 1536), shape(2, 256, kind=F32), shape(2, 256, kind=F32),
            shape(256, 768), shape(256, 1152), shape(352, 1152),
        ],
        compiler_params=PARAMS,
    )(block_w0, block_w1, block_b0, block_b1, mid0, mid1, fin0, fin1)

    vmem = pl.BlockSpec(memory_space=pltpu.VMEM)
    f32 = lambda *dims: pltpu.VMEM(dims, F32)
    bf = lambda *dims: pltpu.VMEM(dims, BF)
    ready = (q0, q1, d01, d02, d12, fin0, fin1, down_fin2[0].T, up_w3[0], up_w2[0], block_w2)
    far = (block_w3,)
    outs = pl.pallas_call(
        main,
        out_shape=[shape(48, 64, 64), shape(32, 32, 96), shape(16, 16, 192), shape(8, 8, 384)],
        in_specs=[vmem] * 24 + [pl.BlockSpec(memory_space=pltpu.HBM)],
        scratch_shapes=[bf(*w.shape) for w in far]
        + [
            f32(2, 1616, 128), f32(2, 1536, 128), f32(2, 1536, 128), bf(1600, 768), bf(1728, 384),
            f32(1728, 128), f32(1760, 128), bf(2, 18 * 32, 384), f32(2, 544, 128), f32(544, 48), bf(64, 432),
            f32(2, 976, 128), f32(2, 928, 128), f32(2, 896, 128), bf(960, 768), bf(2, 18 * 32, 384),
            f32(2, 544, 128), f32(544, 96), bf(64, 864),
            f32(2, 688, 128), f32(2, 624, 128), f32(2, 576, 128), bf(608, 1728), bf(64, 1728),
            f32(3, 208, 128), f32(3, 176, 128), f32(3, 128, 128), bf(192, 1152),
            f32(1024, 48), f32(256, 48), f32(256, 96), f32(1024, 96), f32(256, 128),
            bf(1024, 96), f32(4, 64, 128), f32(3840, 64), f32(80, 48), f32(2, 2, 48, 128), f32(1056, 128),
            pltpu.SemaphoreType.DMA((1,)),
        ],
        compiler_params=MAIN_PARAMS,
    )(*maps, above, below, cl, cr, c0, c1, block_b2, block_b3, up_w1[0], *ready, *far)
    return (outs[0],) + tuple(o.transpose(2, 0, 1) for o in outs[1:])


def solution(mesh):
    tile = P(None, "ty", "tx")
    return jax.shard_map(
        per_device,
        mesh=mesh,
        in_specs=(tile,) * 4 + (P(),) * 16,
        out_specs=(tile,) * 4,
        check_vma=False,
    )
```

```python
import functools

import jax
import jax.numpy as jnp
from jax import lax
from jax.experimental import pallas as pl
from jax.experimental.pallas import tpu as pltpu
from jax.sharding import PartitionSpec as P

BF = jnp.bfloat16
F32 = jnp.float32
TILE = (64, 32, 16, 8)
CHAN = (48, 96, 192, 384)
LEAD = (9, 5, 3, 2)
EXT = (75, 39, 21, 12)
PITCH = (80, 48, 32, 16)
TALL = (80, 48, 32, 16)
GROUP = (16, 16, 16, 8)
DOWN_ROWS, UP_ROWS = 592, 240
RIGHT_ROWS, LEFT_ROWS = 928, 400
PARAMS = pltpu.CompilerParams(vmem_limit_bytes=16 * 2**20)
MAIN_PARAMS = pltpu.CompilerParams(vmem_limit_bytes=39 * 2**20)


def spans(chan):
    return [(lo, min(lo + 128, chan)) for lo in range(0, chan, 128)]


def put_packed(ref, at, value, branch, split):
    if branch == 0:
        ref[at : at + split, 0:48] = value[:split]
        ref[at : at + value.shape[0] - split, 64:112] = value[split:]
        return at + split
    for lo, hi in spans(CHAN[branch]):
        ref[at : at + value.shape[0], 0 : hi - lo] = value[:, lo:hi]
        at += value.shape[0]
    return at


def take_packed(ref, at, count, branch, split):
    if branch == 0:
        return jnp.concatenate(
            [ref[at : at + split, 0:48], ref[at : at + count - split, 64:112]], axis=0
        ), at + split
    parts = []
    for lo, hi in spans(CHAN[branch]):
        parts.append(ref[at : at + count, 0 : hi - lo])
        at += count
    return (parts[0] if len(parts) == 1 else jnp.concatenate(parts, axis=1)), at


def flat_rows(ref, lo, hi, branch):
    side = TILE[branch]
    value = ref[lo:hi].astype(F32)
    return value.reshape((hi - lo) * side, CHAN[branch]).astype(BF)


def pack_rows(f0, f1, f2, f3, down, up):
    at = 0
    for b, f in enumerate((f0, f1, f2, f3)):
        at = put_packed(down, at, flat_rows(f, TILE[b] - LEAD[b], TILE[b], b), b, 288)
    at = 0
    for b, f in enumerate((f0, f1, f2, f3)):
        at = put_packed(up, at, flat_rows(f, 0, 2, b), b, 64)


def pack_cols(f0, f1, f2, f3, above, below, right, left, work):
    down_at = up_at = right_at = left_at = 0
    for b, f in enumerate((f0, f1, f2, f3)):
        side, lead, chan, group = TILE[b], LEAD[b], CHAN[b], GROUP[b]
        high, down_at = take_packed(above, down_at, lead * side, b, 288)
        low, up_at = take_packed(below, up_at, 2 * side, b, 64)
        parts = (
            (high.astype(F32).reshape(lead, side, chan), 0, lead),
            (f[...].astype(F32).reshape(side, side, chan), lead, side),
            (low.astype(F32).reshape(2, side, chan), lead + side, 2),
        )
        for last in (True, False):
            cut = slice(side - group, side) if last else slice(0, group)
            for value, start, count in parts:
                edge = value[:, cut].reshape(count * group, chan)
                for s, (lo, hi) in enumerate(spans(chan)):
                    work[s, start * group : (start + count) * group, 0 : hi - lo] = edge[:, lo:hi]
            columns = range(group - lead, group) if last else range(2)
            cols = []
            for k in columns:
                planes = [
                    work[s, pl.ds(k, TALL[b], stride=group), 0 : hi - lo]
                    for s, (lo, hi) in enumerate(spans(chan))
                ]
                cols.append([p.astype(BF) for p in planes])
            target, at = (right, right_at) if last else (left, left_at)
            if b == 0:
                half = 5 if last else 1
                for i, (col,) in enumerate(cols):
                    place = at + (i if i < half else i - half) * TALL[0]
                    lane = 0 if i < half else 64
                    target[place : place + TALL[0], lane : lane + 48] = col
                at += half * TALL[0]
            else:
                for s, (lo, hi) in enumerate(spans(chan)):
                    for col in cols:
                        target[at : at + TALL[b], 0 : hi - lo] = col[s]
                        at += TALL[b]
            if last:
                right_at = at
            else:
                left_at = at


def clear_edges(place, planes, per, pitch, height, breadth, lead, trail):
    groups = -(-height // per)

    def rows(lo, count):
        for r in range(lo, lo + count):
            spot = slice(r // per * pitch, (r // per + 1) * pitch)
            if per == 4:
                lane = 64 * (r % 2)
                planes[r % 4 // 2][spot, lane : lane + 64] = jnp.zeros((pitch, 64), F32)
            else:
                for ref in [planes[r % 2]] if per == 2 else planes:
                    ref[spot, :] = jnp.zeros((pitch, ref.shape[1]), F32)

    def cols(lo, count):
        for ref in planes:
            for k in range(lo, lo + count):
                ref[pl.ds(k, groups, stride=pitch), :] = jnp.zeros((groups, ref.shape[1]), F32)

    if lead:
        pl.when(place[0] == 0)(lambda: rows(0, lead))
        pl.when(place[1] == 0)(lambda: cols(0, lead))
    if trail:
        pl.when(place[0] == 7)(lambda: rows(height - trail, trail))
        pl.when(place[1] == 7)(lambda: cols(breadth - trail, trail))


def prepare(w0, w1, b0, b1, mid0, mid1, fin0, fin1, q0, q1, c0, c1, d01, d02, d12):
    for out in (q0, q1, c0, c1):
        out[...] = jnp.zeros_like(out)
    for w, q, bias, c, chan, per, slot in ((w0, q0, b0, c0, 48, 4, 64), (w1, q1, b1, c1, 96, 2, 128)):
        for j in range(per):
            c[:, j * slot : j * slot + chan] = bias[...]
            for dy in range(3):
                more, r = divmod(j + dy, per)
                for dx in range(3):
                    lane = more * 768 + dx * 256 + r * slot
                    tap = (dy * 3 + dx) * chan
                    for i in range(2):
                        q[i, j * slot : j * slot + chan, lane : lane + chan] = w[i, :, tap : tap + chan]


    for out in (d01, d02, d12):
        out[...] = jnp.zeros_like(out)
    for tap in range(9):
        dy, dx = divmod(tap, 3)
        cut = slice(tap * 48, tap * 48 + 48)
        lane = dy // 2 * 384 + dx * 128 + dy % 2 * 64
        d01[0:96, lane : lane + 48] = fin0[0:96, cut]
        d01[128:176, lane : lane + 48] = mid0[0, :, cut]
        d01[192:240, lane : lane + 48] = mid0[1, :, cut]
        lane = dy * 384 + dx * 128
        d02[0:192, lane : lane + 48] = fin0[96:288, cut]
        d02[192:240, lane + 64 : lane + 112] = mid0[2, :, cut]
        cut = slice(tap * 96, tap * 96 + 96)
        d12[0:192, lane : lane + 96] = fin1[0:192, cut]
        d12[256:352, lane : lane + 96] = mid1[:, cut]


def dot_nt(x, w):
    return lax.dot_general(x, w, (((1,), (1,)), ((), ())), preferred_element_type=F32)


def rounded(x):
    return x.astype(BF).astype(F32)


PER = (4, 2, 1, 1)


def main(f0, f1, f2, f3, above, below, cl, cr, b0, b1, b2, b3, u1, *rest):
    ready, far, rest = rest[:11], rest[11:12], rest[12:]
    outs, near, scratch = rest[:4], rest[4:5], rest[5:-1]
    main_body(
        f0, f1, f2, f3, above, below, cl, cr, b0, b1, b2, b3, u1, ready, far, near, rest[-1], *outs, *scratch
    )


def main_body(
    f0, f1, f2, f3, above, below, cl, cr, b0, b1, b2, b3, u1, ready, far, near, sems,
    j0, j1, j2, j3,
    x0, h0, a0, s0, t0, v01, v0, ta, vv02, n03, g03,
    x1, h1, a1, s1, t1, vv12, m13, g13,
    x2, h2, a2, s2, g23,
    x3, h3, a3, s3,
    z1, z2, y2, y1, wide, c1, mcol, jt, col_in, col_out, zw,
):
    copies = [pltpu.make_async_copy(a, b, sems.at[i]) for i, (a, b) in enumerate(zip(far, near))]
    for copy in copies:
        copy.start()
    q0, q1, d01, d02, d12, fin0, fin1, fin2, u3, u2, w2 = ready
    w3 = near[0]
    place = (lax.axis_index("ty"), lax.axis_index("tx"))
    feats = (f0, f1, f2, f3)
    two = lambda ref: [ref.at[0], ref.at[1]]
    three = lambda ref: [ref.at[i] for i in range(3)]
    xs = (two(x0), two(x1), two(x2), three(x3))
    hs = (two(h0), two(h1), two(h2), three(h3))
    as_ = (two(a0), two(a1), two(a2), three(a3))
    x0[...] = jnp.zeros_like(x0)
    x1[...] = jnp.zeros_like(x1)

    def put_row(b, r, row):
        side, lead, pitch = TILE[b], LEAD[b], PITCH[b]
        spot = pl.ds(r // PER[b] * pitch + lead, side)
        if b == 0:
            lane = 64 * (r % 2)
            x0[r % 4 // 2, spot, lane : lane + 48] = row
        elif b == 1:
            x1[r % 2, spot, 0:96] = row
        else:
            for s, (lo, hi) in enumerate(spans(CHAN[b])):
                xs[b][s][spot, 0 : hi - lo] = row[:, lo:hi]

    def assemble(b, ats):
        side, lead, chan, pitch = TILE[b], LEAD[b], CHAN[b], PITCH[b]
        down_at, up_at, right_at, left_at = ats
        high, down_at = take_packed(above, down_at, lead * side, b, 288)
        low, up_at = take_packed(below, up_at, 2 * side, b, 64)
        for value, start, count in ((high, 0, lead), (low, lead + side, 2)):
            for y in range(count):
                put_row(b, start + y, value[y * side : (y + 1) * side].astype(F32))
        for y in range(side):
            put_row(b, lead + y, feats[b][y].astype(F32))
        for ref, at, count, begin, half in ((cl, right_at, lead, 0, 5), (cr, left_at, 2, lead + side, 1)):
            if b == 0:
                for i in range(count):
                    spot = at + (i if i < half else i - half) * TALL[0]
                    lane = 0 if i < half else 64
                    col_in[...] = ref[spot : spot + TALL[0], lane : lane + 48].astype(F32)
                    for j in range(4):
                        n = (EXT[0] - j + 3) // 4
                        lane = 64 * (j % 2)
                        col_out[i % 2, j // 2, 0:n, lane : lane + 48] = col_in[pl.ds(j, n, stride=4), :]
                    for s in range(2):
                        x0[s, pl.ds(begin + i, 19, stride=pitch), :] = col_out[i % 2, s, 0:19, :]
                at += half * TALL[0]
            else:
                for s, (lo, hi) in enumerate(spans(chan)):
                    for i in range(count):
                        col = ref[at : at + TALL[b], 0 : hi - lo].astype(F32)
                        at += TALL[b]
                        if b == 1:
                            col_out[0, 0, 0 : TALL[1], 0:96] = col
                            for j in range(2):
                                n = (EXT[1] - j + 1) // 2
                                x1[j, pl.ds(begin + i, n, stride=pitch), :] = col_out[0, 0, pl.ds(j, n, stride=2), :]
                        else:
                            xs[b][s][pl.ds(begin + i, EXT[b], stride=pitch), 0 : hi - lo] = col[: EXT[b]]
            if ref is cl:
                right_at = at
            else:
                left_at = at
        clear_edges(place, xs[b], PER[b], pitch, EXT[b], EXT[b], lead, 2)
        return down_at, up_at, right_at, left_at

    col_out[...] = jnp.zeros_like(col_out)
    ats = (0, 0, 0, 0)
    for b in range(4):
        ats = assemble(b, ats)

    def steps(rows, count, body):
        step = rows // count
        if count == 1:
            body(0, step)
            return

        @pl.loop(0, count)
        def _(i):
            body(pl.multiple_of(i * step, 16), step)

    def spread(planes, target, rows, count, slot):
        def body(p, step):
            for dx in range(3):
                for s, plane in enumerate(planes):
                    piece = plane[pl.ds(p + dx, step), :].astype(BF)
                    target[pl.ds(p, step), dx * slot + s * 128 : dx * slot + s * 128 + 128] = piece

        steps(rows, count, body)

    def side_by_side(planes, target, rows):
        for tap in range(9):
            at = tap // 3 * 32 + tap % 3
            piece = jnp.concatenate(
                [planes[0][at : at + rows, :], planes[1][at : at + rows, 0:64]], axis=1
            )
            target[0:rows, tap * 192 : tap * 192 + 192] = piece.astype(BF)

    def block(b, weight, bias, source, counts):
        pitch, chan, lead, per = PITCH[b], CHAN[b], LEAD[b], PER[b]
        reach = (2, 2, 1, 3)[b]
        slot = 384 if b == 3 else 256

        def conv(i, p, step):
            taps = [source[pl.ds(p + k * pitch, step), :] for k in range(reach)]
            return dot_nt(jnp.concatenate(taps, axis=1), weight[i]) + bias[i : i + 1, :]

        def cuts(total):
            return [(s, lo, hi) for s, (lo, hi) in enumerate(spans(total.shape[1]))]

        def inner(p, step):
            value = jnp.maximum(conv(0, p, step), 0.0)
            for s, lo, hi in cuts(value):
                hs[b][s][pl.ds(p, step), 0 : hi - lo] = value[:, lo:hi]

        def outer(p, step):
            total = conv(1, p, step)
            for s, lo, hi in cuts(total):
                if per == 4:
                    kept = x0[1 - s, pl.ds(p + s * pitch + 2, step), :]
                elif per == 2:
                    kept = x1[s, pl.ds(p + pitch + 2, step), :]
                else:
                    kept = xs[b][s][pl.ds(p + 2 * pitch + 2, step), 0 : hi - lo]
                value = rounded(jnp.maximum(kept + total[:, lo:hi], 0.0))
                as_[b][s][pl.ds(p, step), 0 : hi - lo] = value

        inner_rows = -(-(EXT[b] - 2) // per) * pitch
        outer_rows = -(-(EXT[b] - 4) // per) * pitch
        extra = (reach - 1) * pitch
        if b == 2:
            side_by_side(xs[b], source, inner_rows)
        else:
            spread(xs[b], source, inner_rows + extra, counts[0], slot)
        steps(inner_rows, counts[1], inner)
        clear_edges(place, hs[b], per, pitch, EXT[b] - 2, EXT[b] - 2, lead - 1, 1)
        if b == 2:
            side_by_side(hs[b], source, outer_rows)
        else:
            spread(hs[b], source, outer_rows + extra, counts[2], slot)
        steps(outer_rows, counts[3], outer)
        clear_edges(place, as_[b], per, pitch, EXT[b] - 4, EXT[b] - 4, lead - 2, 0)

    block(0, q0, b0, s0, (1, 1, 1, 1))
    block(1, q1, b1, s1, (1, 1, 1, 1))
    block(2, w2, b2, s2, (1, 1, 1, 1))
    copies[0].wait()
    block(3, w3, b3, s3, (1, 1, 1, 1))

    for pair in range(36):
        for dx in range(3):
            piece = a0[pair % 2, pl.ds(pair // 2 * 80 + dx, 48, stride=2), :]
            t0[pair * 48 : pair * 48 + 48, dx * 128 : dx * 128 + 128] = piece.astype(BF)

    def first(p, step):
        both = jnp.concatenate([t0[pl.ds(p, step), :], t0[pl.ds(p + 48, step), :]], axis=1)
        total = dot_nt(both, d01[...])
        v01[pl.ds(p, step), :] = rounded(total[:, :128])
        v0[pl.ds(p, step), :] = rounded(jnp.maximum(total[:, 128:], 0.0))

    steps(35 * 48, 1, first)
    clear_edges(place, [v0], 1, 48, 35, 35, 3, 0)

    for row in range(35):
        spot = slice(row // 2 * 32, row // 2 * 32 + 32)
        for dx in range(3):
            lane = slice(dx * 128, dx * 128 + 128)
            ta[row % 2, spot, lane] = v0[pl.ds(row * 48 + dx, 32, stride=2), :].astype(BF)
            piece = a1[row % 2, pl.ds(row // 2 * 48 + dx, 32, stride=2), :]
            t1[row % 2, spot, lane] = piece.astype(BF)

    def second(source, p, n, weight):
        taps = [source[dy % 2, p + dy // 2 * 32 : p + dy // 2 * 32 + n, :] for dy in range(3)]
        return dot_nt(jnp.concatenate(taps, axis=1), weight[...])

    for p, n in ((0, 272), (272, 272)):
        cut = slice(p, p + n)
        total = second(ta, p, n, d02)
        vv02[0, cut, :] = rounded(total[:, :128])
        vv02[1, cut, 0:64] = rounded(total[:, 128:192])
        n03[cut, :] = rounded(jnp.maximum(total[:, 192:240], 0.0))
        total = second(t1, p, n, d12)
        vv12[0, cut, :] = rounded(total[:, :128])
        vv12[1, cut, 0:64] = rounded(total[:, 128:192])
        m13[cut, :] = rounded(jnp.maximum(total[:, 256:352], 0.0))

    clear_edges(place, [n03], 1, 32, 17, 17, 1, 0)
    clear_edges(place, [m13], 1, 32, 17, 17, 1, 0)

    def gathered(ref, width, dy, dx):
        return jnp.concatenate(
            [ref[pl.ds((2 * i + dy) * 32 + dx, 8, stride=2), 0:width] for i in range(8)], axis=0
        ).astype(BF)

    for tap in range(9):
        dy, dx = divmod(tap, 3)
        g03[:, tap * 48 : tap * 48 + 48] = gathered(n03, 48, dy, dx)
        g13[:, tap * 96 : tap * 96 + 96] = gathered(m13, 96, dy, dx)
        for s, (lo, hi) in enumerate(spans(192)):
            g23[:, tap * 192 + lo : tap * 192 + hi] = gathered(a2.at[s], hi - lo, dy, dx)
    t03 = dot_nt(g03[...], fin0[288:672, :])
    t13 = dot_nt(g13[...], fin1[192:576, :])
    t23 = jnp.dot(g23[...], fin2[...], preferred_element_type=F32)

    c3 = [
        jnp.concatenate([a3[s, y * 16 : y * 16 + 8, :] for y in range(8)], axis=0) for s in range(3)
    ]
    c3 = jnp.concatenate(c3, axis=1)
    three = jnp.maximum(c3 + rounded(t03) + rounded(t13) + rounded(t23), 0.0)
    j3[...] = three.reshape(8, 8, 384).astype(BF)

    c3b = c3.astype(BF)
    t30 = rounded(dot_nt(c3b, u3[0:48, :]))
    t31 = rounded(dot_nt(c3b, u3[48:144, :]))
    t32 = rounded(dot_nt(c3b, u3[144:336, :]))
    c2 = [
        jnp.concatenate([a2[s, pl.ds((y + 1) * 32 + 1, 16), 0 : hi - lo] for y in range(16)], axis=0)
        for s, (lo, hi) in enumerate(spans(192))
    ]
    c2 = jnp.concatenate(c2, axis=1)
    c2b = c2.astype(BF)
    t20 = rounded(dot_nt(c2b, u2[0:48, :]))
    t21 = rounded(dot_nt(c2b, u2[48:144, :]))

    def doubled(target, small, side, lanes):
        for y in range(side):
            row = small[y * side : (y + 1) * side]
            for odd in range(2):
                for right in range(2):
                    target[pl.ds((2 * y + odd) * 2 * side + right, side, stride=2), 0:lanes] = row

    for s, (lo, hi) in enumerate(spans(192)):
        doubled(wide, t32[:, lo:hi], 8, hi - lo)
        for y in range(16):
            t02 = vv02[s, pl.ds((y + 1) * 32 + 1, 16), 0 : hi - lo]
            t12 = vv12[s, pl.ds((y + 1) * 32 + 1, 16), 0 : hi - lo]
            keep = c2[y * 16 : (y + 1) * 16, lo:hi]
            row = keep + t02 + t12 + wide[pl.ds(y * 16, 16), 0 : hi - lo]
            j2[y, :, lo:hi] = jnp.maximum(row, 0.0).astype(BF)

    doubled(z2, t30, 8, 48)
    sum2 = z2[...] + t20
    doubled(z1, sum2, 16, 48)
    doubled(y2, t31, 8, 96)
    sum2 = y2[...] + t21
    doubled(y1, sum2, 16, 96)

    for y in range(32):
        row = a1[(y + 3) % 2, pl.ds((y + 3) // 2 * 48 + 3, 32), 0:96]
        c1[y * 32 : y * 32 + 32, :] = row.astype(BF)
    total = z1[...] + rounded(dot_nt(c1[...], u1[...]))
    zw[32:1056, 0:48] = total
    zw[0:1024, 64:112] = total

    def last_rows(m, plane, group, k):
        for right in range(2):
            mcol[k, pl.ds(right, 32, stride=2), :] = zw[pl.ds(m * 32, 32), :]
        zero = a0[plane, pl.ds(group * 80 + 7, 64), :]
        turned = jnp.maximum(zero + mcol[k], 0.0).T
        jt[pl.ds(2 * m + 7, 48, stride=80), :] = turned[0:48]
        jt[pl.ds(2 * m + 8, 48, stride=80), :] = turned[64:112]

    @pl.loop(0, 8, unroll=8)
    def _(i):
        for k in range(4):
            y = 4 * i + k
            spot = pl.ds(pl.multiple_of(y * 32, 32), 32)
            one = a1[(k + 3) % 2, pl.ds((2 * i + (k + 3) // 2) * 48 + 3, 32), 0:96]
            t01 = v01[pl.ds((y + 3) * 48 + 3, 32), 0:96]
            j1[y] = jnp.maximum(one + t01 + y1[spot, :], 0.0).astype(BF)
            last_rows(y, (3 + k) % 2, 2 * i + (3 + k) // 2, k)

    last_rows(32, 1, 17, 0)

    @pl.loop(0, 6, unroll=6)
    def _(i):
        for c in range(8):
            c = 8 * i + c
            j0[c] = jt[pl.ds(pl.multiple_of(c * 80 + 8, 8), 64), :].astype(BF)


def ring(x, axis, by):
    n = lax.axis_size(axis)
    return lax.ppermute(x, axis, [(i, (i + by) % n) for i in range(n)])


def shape(*dims, kind=BF):
    return jax.ShapeDtypeStruct(dims, kind)


def per_device(
    feat0, feat1, feat2, feat3,
    block_w0, block_w1, block_w2, block_w3,
    block_b0, block_b1, block_b2, block_b3,
    up_w1, up_w2, up_w3,
    down_mid0, down_mid1, down_fin0, down_fin1, down_fin2,
):
    maps = [f.transpose(1, 2, 0) for f in (feat0, feat1, feat2, feat3)]
    down, up = pl.pallas_call(
        pack_rows,
        out_shape=[shape(DOWN_ROWS, 128), shape(UP_ROWS, 128)],
        compiler_params=PARAMS,
    )(*maps)
    above, below = ring(down, "ty", 1), ring(up, "ty", -1)
    fin0, fin1, mid0, mid1 = down_fin0[0], down_fin1[0], down_mid0[0], down_mid1[0, 0]
    above, below, fin0 = lax.optimization_barrier((above, below, fin0))
    right, left = pl.pallas_call(
        pack_cols,
        out_shape=[shape(RIGHT_ROWS, 128), shape(LEFT_ROWS, 128)],
        scratch_shapes=[pltpu.VMEM((3, 80 * 16, 128), F32)],
        compiler_params=PARAMS,
    )(*maps, above, below)
    cl, cr = ring(right, "tx", 1), ring(left, "tx", -1)

    q0, q1, c0, c1, d01, d02, d12 = pl.pallas_call(
        prepare,
        out_shape=[
            shape(2, 256, 1536), shape(2, 256, 1536), shape(2, 256, kind=F32), shape(2, 256, kind=F32),
            shape(256, 768), shape(256, 1152), shape(352, 1152),
        ],
        compiler_params=PARAMS,
    )(block_w0, block_w1, block_b0, block_b1, mid0, mid1, fin0, fin1)

    vmem = pl.BlockSpec(memory_space=pltpu.VMEM)
    f32 = lambda *dims: pltpu.VMEM(dims, F32)
    bf = lambda *dims: pltpu.VMEM(dims, BF)
    ready = (q0, q1, d01, d02, d12, fin0, fin1, down_fin2[0].T, up_w3[0], up_w2[0], block_w2)
    far = (block_w3,)
    outs = pl.pallas_call(
        main,
        out_shape=[shape(48, 64, 64), shape(32, 32, 96), shape(16, 16, 192), shape(8, 8, 384)],
        in_specs=[vmem] * 24 + [pl.BlockSpec(memory_space=pltpu.HBM)],
        scratch_shapes=[bf(*w.shape) for w in far]
        + [
            f32(2, 1616, 128), f32(2, 1536, 128), f32(2, 1536, 128), bf(1600, 768), bf(1728, 384),
            f32(1728, 128), f32(1760, 128), bf(2, 18 * 32, 384), f32(2, 544, 128), f32(544, 48), bf(64, 432),
            f32(2, 976, 128), f32(2, 928, 128), f32(2, 896, 128), bf(960, 768), bf(2, 18 * 32, 384),
            f32(2, 544, 128), f32(544, 96), bf(64, 864),
            f32(2, 688, 128), f32(2, 624, 128), f32(2, 576, 128), bf(608, 1728), bf(64, 1728),
            f32(3, 208, 128), f32(3, 176, 128), f32(3, 128, 128), bf(192, 1152),
            f32(1024, 48), f32(256, 48), f32(256, 96), f32(1024, 96), f32(256, 128),
            bf(1024, 96), f32(4, 64, 128), f32(3840, 64), f32(80, 48), f32(2, 2, 48, 128), f32(1056, 128),
            pltpu.SemaphoreType.DMA((1,)),
        ],
        compiler_params=MAIN_PARAMS,
    )(*maps, above, below, cl, cr, c0, c1, block_b2, block_b3, up_w1[0], *ready, *far)
    return (outs[0],) + tuple(o.transpose(2, 0, 1) for o in outs[1:])


def solution(mesh):
    tile = P(None, "ty", "tx")
    return jax.shard_map(
        per_device,
        mesh=mesh,
        in_specs=(tile,) * 4 + (P(),) * 16,
        out_specs=(tile,) * 4,
        check_vma=False,
    )
```
